256 devices in a mesh: pts: 16 (over z, core), row: 4 (over x), col: 4 (over y).
Axes of the slice: x: 4, y: 4, z: 8, core: 2. Of those that a mesh axis runs over, the one named last changes fastest.
Arguments:
- weights: bfloat16 [12, 32768, 256], P(None, ('pts', 'row', 'col')), as said below
- visibility: int32 [4, 32768], P(None, ('pts', 'row', 'col')), may hold values from 0 to 16, as said below
- inverses: bfloat16 [6, 32768], P(None, ('pts', 'row', 'col')), as said below
- grad_points: bfloat16 [3, 32768], P(None, ('pts', 'row', 'col')), may hold values from -6 to 6
- camera_blocks: float32 [4096, 256], P(('pts', 'row')), as said below
- grad_cams: float32 [4096], P(('pts', 'row')), may hold values from -6 to 6
Outputs:
- schur: float32 [4096, 4096], P(('pts', 'row'), 'col')
- reduced_rhs: float32 [4096], P(('pts', 'row'))
- solution: float32 [4096], P(('pts', 'row'))
The draws below stay inside these ranges and needn't reach their ends.
Inputs may be any that keep to these rules, and one draw needn't show every extreme that they name: `weights`: entries of a slot whose visibility entry is 16 are arbitrary. `visibility`: column p lists the camera blocks point p sees: its first c entries are distinct blocks, with 1 <= c <= min(4, 16); the remaining entries are 16 and mark empty slots. `inverses`: rows 0 to 2 hold the diagonal of a symmetric positive definite 3 x 3 matrix, rows 3, 4, 5 its entries (0,1), (0,2), (1,2). `camera_blocks`: the 256 rows of block b hold a symmetric 256 x 256 matrix.
All inputs are finite; a program needn't handle non-finite values.
Results may differ from the reference program's by a relative error of at most 0.0048.
Values may be sent and summed in bfloat16 or wider, within the bound.
No kernel may reach another device: no remote copies, remote signals or barrier semaphores. Data moves between devices by JAX's collectives and lax.ppermute only.
A program may use at most 64 MiB of HBM per device.

```python
import math
import jax
import jax.numpy as jnp
from jax import lax

BW = 256
K = 4
ITERS = 3
NB = 16
NC = 4096
POINTS = 32768


def draw_weights(key, part):
    key_noise, key_sign = jax.random.split(key, 2)
    scale_w = (4.0 * (POINTS // NB) * (K + 1)) ** (-0.5)
    signs = jnp.where(jax.random.bernoulli(key_sign, 0.5, (BW,)), 1.0, -1.0).astype(jnp.float32)
    noise = jnp.clip(jax.random.normal(key_noise, (3 * K, POINTS, BW), jnp.float32), -6.0, 6.0)
    values = (noise + 1.2 * signs[None, None, :]) * scale_w
    return values.astype(jnp.float32).astype(jnp.bfloat16)


def draw_visibility(key, part):
    key_count, key_base, key_stride = jax.random.split(key, 3)
    counts = jax.random.randint(key_count, (POINTS,), 1, min(K, NB) + 1)
    base_blk = jax.random.randint(key_base, (POINTS,), 0, NB)
    strides = 2 * jax.random.randint(key_stride, (POINTS,), 0, max(NB // 2, 1)) + 1
    slots = jnp.arange(K, dtype=jnp.int32)[:, None]
    blocks = (base_blk[None, :] + slots * strides[None, :]) % NB
    return jnp.where(slots < counts[None, :], blocks, NB).astype(jnp.int32)


def draw_inverses(key, part):
    key_diag, key_off = jax.random.split(key, 2)
    diag = jax.random.uniform(key_diag, (3, POINTS), jnp.float32, 0.5, 2.0)
    off = jax.random.uniform(key_off, (3, POINTS), jnp.float32, -0.24, 0.24)
    return jnp.concatenate([diag, off], 0).astype(jnp.bfloat16)


def draw_camera_blocks(key, part):
    key_noise, key_diag = jax.random.split(key, 2)
    noise = jax.random.normal(key_noise, (NB, BW, BW), jnp.float32) * 0.03
    sym = (noise + jnp.swapaxes(noise, 1, 2)) * 0.5
    diag = jax.random.uniform(key_diag, (NB, BW), jnp.float32, 1.5, 4.0)
    eye_bw = jnp.eye(BW, dtype=jnp.float32)
    return (sym + eye_bw[None, :, :] * diag[:, :, None]).reshape(NB * BW, BW).astype(jnp.float32)


def block_scale(own_key, extent, pieces, low, high):
    def one(axis_at, parts):
        draws = jax.random.uniform(jax.random.fold_in(jax.random.fold_in(own_key, 6), axis_at), (parts,), jnp.float32, low / len(pieces), high / len(pieces))
        return jnp.repeat(jnp.exp(draws), extent[axis_at] // parts).reshape((-1,) + (1,) * (len(extent) - axis_at - 1))

    level = one(*pieces[0])
    for cut in pieces[1:]:
        level = level * one(*cut)
    return level


def centred(key, shape, spread, bound, pieces=(), held_as=jnp.bfloat16):
    values = spread * jax.random.normal(key, shape, jnp.float32)
    if pieces:
        values = values * block_scale(key, shape, pieces, -0.22, 0.18)
    return jnp.clip(values, -bound, bound).astype(held_as)


def setup_inputs(seed: int = 0) -> dict:
    key_of = jax.random.split(jax.random.key(seed), 7)
    weights = draw_weights(jax.random.fold_in(key_of[6], 71), 0)
    visibility = draw_visibility(jax.random.fold_in(key_of[6], 71), 0)
    inverses = draw_inverses(jax.random.fold_in(key_of[6], 71), 0)
    grad_points = centred(key_of[3], (3, POINTS), 1.0, 6.0, ((1, 256),))
    camera_blocks = draw_camera_blocks(jax.random.fold_in(key_of[6], 71), 0)
    grad_cams = centred(key_of[5], (NC,), 1.0, 6.0, ((0, 64),), jnp.float32)
    return {"weights": weights, "visibility": visibility, "inverses": inverses, "grad_points": grad_points, "camera_blocks": camera_blocks, "grad_cams": grad_cams}


def apply_inverse(coefs, rows):
    target_shape = coefs.shape[1:] + (1,) * (rows.ndim - 2)
    entries = [coefs[entry].reshape(target_shape) for entry in range(6)]
    first = entries[0] * rows[0] + entries[3] * rows[1] + entries[4] * rows[2]
    second = entries[3] * rows[0] + entries[1] * rows[1] + entries[5] * rows[2]
    third = entries[4] * rows[0] + entries[5] * rows[1] + entries[2] * rows[2]
    return jnp.stack([first, second, third], 0)

def minres_steps(operate, inner, rhs_vec):
    beta_first = jnp.sqrt(inner(rhs_vec, rhs_vec))
    r_older = rhs_vec
    r_old = rhs_vec
    lanczos = rhs_vec
    beta_old = jnp.float32(0.0)
    beta_now = beta_first
    d_bar = jnp.float32(0.0)
    eps_now = jnp.float32(0.0)
    phi_bar = beta_first
    cos_now = jnp.float32(-1.0)
    sin_now = jnp.float32(0.0)
    w_now = jnp.zeros_like(rhs_vec)
    w_old = jnp.zeros_like(rhs_vec)
    answer = jnp.zeros_like(rhs_vec)
    for turn in range(ITERS):
        v_now = lanczos / beta_now
        lanczos = operate(v_now)
        if turn > 0:
            lanczos = lanczos - beta_now / beta_old * r_older
        alpha_now = inner(v_now, lanczos)
        lanczos = lanczos - alpha_now / beta_now * r_old
        r_older = r_old
        r_old = lanczos
        beta_old = beta_now
        beta_now = jnp.sqrt(inner(lanczos, lanczos))
        eps_old = eps_now
        delta_now = cos_now * d_bar + sin_now * alpha_now
        g_bar = sin_now * d_bar - cos_now * alpha_now
        eps_now = sin_now * beta_now
        d_bar = -cos_now * beta_now
        gamma_now = jnp.sqrt(g_bar * g_bar + beta_now * beta_now)
        cos_now = g_bar / gamma_now
        sin_now = beta_now / gamma_now
        phi_now = cos_now * phi_bar
        phi_bar = sin_now * phi_bar
        w_older = w_old
        w_old = w_now
        w_now = (v_now - eps_old * w_older - delta_now * w_old) / gamma_now
        answer = answer + phi_now * w_now
    return answer

def reference(weights, visibility, inverses, grad_points, camera_blocks, grad_cams):
    block_len = math.gcd(POINTS, 512)
    contract = (((0, 1), (0, 1)), ((), ()))

    def one_block(carry, index_blk):
        g_acc, r_acc = carry
        offset_pts = index_blk * block_len
        w_blk = lax.dynamic_slice_in_dim(weights, offset_pts, block_len, 1).reshape(K, 3, block_len, BW)
        vis_blk = lax.dynamic_slice_in_dim(visibility, offset_pts, block_len, 1)
        inv_blk = lax.dynamic_slice_in_dim(inverses, offset_pts, block_len, 1).astype(jnp.float32)
        grad_blk = lax.dynamic_slice_in_dim(grad_points, offset_pts, block_len, 1).astype(jnp.float32)
        mask_all = (vis_blk[:, :, None] == jnp.arange(NB, dtype=jnp.int32)[None, None, :]).astype(jnp.float32)
        y_rows = jnp.einsum('kpb,kapi->apbi', mask_all, w_blk.astype(jnp.float32)).reshape(3, block_len, NC)
        z_rows = apply_inverse(inv_blk, y_rows).astype(jnp.bfloat16)
        z_rows = lax.optimization_barrier(z_rows).astype(jnp.float32)
        e_rows = apply_inverse(inv_blk, grad_blk).astype(jnp.bfloat16)
        e_rows = lax.optimization_barrier(e_rows).astype(jnp.float32)
        g_acc = g_acc + lax.dot_general(y_rows, z_rows, contract, precision=lax.Precision.HIGHEST)
        r_acc = r_acc + lax.dot_general(y_rows, e_rows, contract, precision=lax.Precision.HIGHEST)
        return ((g_acc, r_acc), None)
    init = (jnp.zeros((NC, NC), jnp.float32), jnp.zeros((NC,), jnp.float32))
    (g_total, r_total), unused = lax.scan(one_block, init, jnp.arange(POINTS // block_len, dtype=jnp.int32))
    ublocks = camera_blocks.reshape(NB, BW, BW)
    eye_nb = jnp.eye(NB, dtype=jnp.float32)
    ufull = (eye_nb[:, None, :, None] * ublocks[:, :, None, :]).reshape(NC, NC)
    schur = ufull - g_total
    reduced_rhs = grad_cams - r_total

    def operate(vector):
        return jnp.dot(schur, vector, precision=lax.Precision.HIGHEST)

    def inner(first, second):
        return jnp.sum(first * second)
    solution = minres_steps(operate, inner, reduced_rhs)
    return (schur, reduced_rhs, solution)
```

```python
import functools

import jax
import jax.numpy as jnp
from jax import lax
from jax.experimental import pallas as pl
from jax.experimental.pallas import tpu as pltpu
from jax.sharding import PartitionSpec as P

ITERS = 3
NT = (((1,), (1,)), ((), ()))
AUX = 16


def total(first, second):
    return jnp.sum(jnp.sum(first * second, axis=1, keepdims=True), axis=0, keepdims=True)


def minres(rhs_vec, products):
    beta_first = jnp.sqrt(total(rhs_vec, rhs_vec))
    r_older = rhs_vec
    r_old = rhs_vec
    lanczos = rhs_vec
    zero = jnp.zeros_like(beta_first)
    beta_old = zero
    beta_now = beta_first
    d_bar = zero
    eps_now = zero
    phi_bar = beta_first
    cos_now = zero - 1.0
    sin_now = zero
    w_now = jnp.zeros_like(rhs_vec)
    w_old = jnp.zeros_like(rhs_vec)
    answer = jnp.zeros_like(rhs_vec)
    for turn in range(ITERS):
        v_now = lanczos / beta_now
        if turn == len(products):
            return v_now
        lanczos = products[turn]
        if turn > 0:
            lanczos = lanczos - beta_now / beta_old * r_older
        alpha_now = total(v_now, lanczos)
        lanczos = lanczos - alpha_now / beta_now * r_old
        beta_old = beta_now
        beta_now = jnp.sqrt(total(lanczos, lanczos))
        r_older = r_old
        r_old = lanczos
        eps_old = eps_now
        delta_now = cos_now * d_bar + sin_now * alpha_now
        g_bar = sin_now * d_bar - cos_now * alpha_now
        eps_now = sin_now * beta_now
        d_bar = -cos_now * beta_now
        gamma_now = jnp.sqrt(g_bar * g_bar + beta_now * beta_now)
        cos_now = g_bar / gamma_now
        sin_now = beta_now / gamma_now
        phi_now = cos_now * phi_bar
        phi_bar = sin_now * phi_bar
        w_older = w_old
        w_old = w_now
        w_now = (v_now - eps_old * w_older - delta_now * w_old) / gamma_now
        answer = answer + phi_now * w_now
    return answer


def apply_inverse(inv, rows):
    return (
        inv[0] * rows[0] + inv[3] * rows[1] + inv[4] * rows[2],
        inv[3] * rows[0] + inv[1] * rows[1] + inv[5] * rows[2],
        inv[4] * rows[0] + inv[5] * rows[1] + inv[2] * rows[2],
    )


def slot_masks(vis, blocks):
    points = vis.shape[1]
    ids = lax.broadcasted_iota(jnp.int32, (blocks, points), 0)
    return [(vis[k : k + 1, :] == ids).astype(jnp.float32) for k in range(vis.shape[0])]


def prepare_kernel(slots, blocks, w_ref, vis_ref, inv_ref, grad_ref, cams_ref, send_ref, zw_ref, part_ref):
    points = vis_ref.shape[1]
    width = w_ref.shape[1]
    inv = inv_ref[...].astype(jnp.float32)
    inv_rows = [inv[e : e + 1, :] for e in range(6)]
    grad = grad_ref[...].astype(jnp.float32)
    vis = vis_ref[...]
    for k in range(slots):
        turned = []
        for a in range(3):
            at = 3 * k + a
            t = jnp.transpose(w_ref[at * points : (at + 1) * points, :].astype(jnp.float32))
            turned.append(t)
            send_ref[at * width : (at + 1) * width, :] = t.astype(jnp.bfloat16)
        for a, z in enumerate(apply_inverse(inv_rows, turned)):
            at = 3 * k + a
            zw_ref[:, at * points : (at + 1) * points] = z.astype(jnp.bfloat16)
    pad = jnp.zeros((AUX - slots - 6, points), jnp.float32)
    aux = jnp.concatenate([vis.astype(jnp.float32), inv, pad], axis=0)
    send_ref[3 * slots * width :, :] = aux.astype(jnp.bfloat16)
    masks = slot_masks(vis, blocks)
    moved = apply_inverse(inv_rows, [grad[a : a + 1, :] for a in range(3)])
    moved = [e.astype(jnp.bfloat16).astype(jnp.float32) for e in moved]
    lhs = jnp.concatenate([masks[k] * moved[a] for k in range(slots) for a in range(3)], axis=1)
    terms = jnp.dot(lhs.astype(jnp.bfloat16), w_ref[...], preferred_element_type=jnp.float32)
    part_ref[...] = cams_ref[...] - terms


def split(x):
    high = x.astype(jnp.bfloat16)
    low = (x - high.astype(jnp.float32)).astype(jnp.bfloat16)
    return high, low


def product_kernel(slots, blocks, n_known, *refs):
    place_ref, vis_ref, w_ref, zw_ref, cam_ref = refs[:5]
    known = refs[5 : 5 + n_known]
    out_ref = refs[5 + n_known]
    points = vis_ref.shape[1]
    v = minres(known[0][...], [r[...] for r in known[1:]])
    masks = slot_masks(vis_ref[...], blocks)
    v2 = jnp.concatenate(split(v), axis=0)
    dots = jnp.dot(v2, zw_ref[...], preferred_element_type=jnp.float32)
    dots = dots[:blocks] + dots[blocks:]
    t = []
    for a in range(3):
        s = None
        for k in range(slots):
            at = 3 * k + a
            term = masks[k] * dots[:, at * points : (at + 1) * points]
            s = term if s is None else s + term
        t.append(jnp.sum(s, axis=0, keepdims=True))
    lhs = jnp.concatenate([masks[k] * t[a] for k in range(slots) for a in range(3)], axis=1)
    lhs2 = jnp.concatenate(split(lhs), axis=0)
    terms = jnp.dot(lhs2, w_ref[...], preferred_element_type=jnp.float32)
    rows = lax.broadcasted_iota(jnp.int32, v.shape, 0)
    own = jnp.where(rows == place_ref[0], v, 0.0)
    cams = jnp.dot(own, cam_ref[...], precision=lax.Precision.HIGHEST, preferred_element_type=jnp.float32)
    out_ref[...] = cams - terms[:blocks] - terms[blocks:]


def answer_kernel(rhs_ref, s1_ref, s2_ref, s3_ref, out_ref):
    out_ref[...] = minres(rhs_ref[...], [s1_ref[...], s2_ref[...], s3_ref[...]])


def tile_kernel(slots, blocks, width, strip, place_ref, got_ref, cam_ref, out_ref, row_ref, col_ref):
    pts_idx, row_idx, col_idx = place_ref[0], place_ref[1], place_ref[2]
    sources, _, points = got_ref.shape
    col_blocks = out_ref.shape[1] // width

    @pl.when(pl.program_id(0) == 0)
    def _():
        out_ref[...] = jnp.zeros_like(out_ref)
        for c in range(col_blocks):

            @pl.when(col_idx * col_blocks + c == pts_idx)
            def _():
                start = pl.multiple_of(pts_idx * strip, strip)
                out_ref[pl.ds(start, strip), c * width : (c + 1) * width] = cam_ref[...]

    base_aux = 3 * slots * width
    for s in range(sources):
        aux = got_ref[s, base_aux : base_aux + AUX, :].astype(jnp.float32)
        vis = [aux[k : k + 1, :] for k in range(slots)]
        inv = [aux[slots + e : slots + e + 1, :] for e in range(6)]

        @pl.loop(0, col_blocks)
        def _(c):
            block = (col_idx * col_blocks + c).astype(jnp.float32)
            picks = [jnp.where(vis[k] == block, 1.0, 0.0).astype(jnp.bfloat16) for k in range(slots)]
            start = pl.multiple_of(c * width, width)
            for h in range(0, width, 64):
                rows = []
                for a in range(3):
                    y = None
                    for k in range(slots):
                        at = (3 * k + a) * width + h
                        term = picks[k] * got_ref[s, at : at + 64, :]
                        y = term if y is None else y + term
                    rows.append(y.astype(jnp.float32))
                for a, z in enumerate(apply_inverse(inv, rows)):
                    at = (a * sources + s) * points
                    col_ref[pl.ds(start + h, 64), at : at + points] = z.astype(jnp.bfloat16)

        @pl.loop(0, blocks)
        def _(b):
            block = b.astype(jnp.float32)
            picks = [jnp.where(vis[k] == block, -1.0, 0.0).astype(jnp.bfloat16) for k in range(slots)]
            start = pl.multiple_of(b * strip, strip)
            for a in range(3):
                y = None
                for k in range(slots):
                    at = pl.multiple_of((3 * k + a) * width + row_idx * strip, strip)
                    term = picks[k] * got_ref[s, pl.ds(at, strip), :]
                    y = term if y is None else y + term
                at = (a * sources + s) * points
                row_ref[pl.ds(start, strip), at : at + points] = y

    step = 256

    @pl.loop(0, out_ref.shape[0] // step)
    def _(m):
        start = pl.multiple_of(m * step, step)
        out_ref[pl.ds(start, step), :] += lax.dot_general(
            row_ref[pl.ds(start, step), :], col_ref[...], NT, preferred_element_type=jnp.float32
        )


def swap(value, axis, size, bit):
    return lax.ppermute(value, axis, [(i, i ^ bit) for i in range(size)])


def tree(values):
    while len(values) > 1:
        values = [values[i] + values[i + 1] for i in range(0, len(values), 2)]
    return values[0]


def all_sum(value, n_pts, n_row, n_col):
    value = value + swap(value, "pts", n_pts, 1)
    for axis, size, unit in (("row", n_row, 1), ("col", n_col, 1), ("pts", n_pts, 2)):
        value = tree([value] + [swap(value, axis, size, b) for b in range(unit, size, unit)])
    return value


def per_device(weights, visibility, inverses, grad_points, camera_blocks, grad_cams):
    n_row = lax.axis_size("row")
    n_col = lax.axis_size("col")
    blocks = lax.axis_size("pts")
    pts_idx = lax.axis_index("pts")
    row_idx = lax.axis_index("row")
    col_idx = lax.axis_index("col")
    slots, points = visibility.shape
    width = weights.shape[2]
    strip = width // n_row
    total_rows = blocks * width
    col_count = total_rows // n_col
    set_rows = blocks * strip
    shards = n_row * n_col
    send_rows = 3 * slots * width + AUX
    place = jnp.stack([pts_idx, row_idx, col_idx]).astype(jnp.int32)
    w_flat = weights.reshape(3 * slots * points, width)
    first_col = (col_idx == 0).astype(jnp.float32)
    lanes = jnp.arange(width, dtype=jnp.int32)[None, :]
    own_lanes = (lanes // strip == row_idx) & (jnp.arange(blocks, dtype=jnp.int32)[:, None] == pts_idx)
    cams_placed = jnp.where(own_lanes, jnp.tile(grad_cams, n_row)[None, :] * first_col, 0.0)
    cam_wide = lax.dynamic_update_slice(
        jnp.zeros((width, width), jnp.float32), camera_blocks * first_col, (row_idx * strip, 0)
    )
    vmem = pl.BlockSpec(memory_space=pltpu.VMEM)
    smem = pl.BlockSpec(memory_space=pltpu.SMEM)
    vec = jax.ShapeDtypeStruct((blocks, width), jnp.float32)

    send, zw, part = pl.pallas_call(
        functools.partial(prepare_kernel, slots, blocks),
        out_shape=(
            jax.ShapeDtypeStruct((send_rows, points), jnp.bfloat16),
            jax.ShapeDtypeStruct((width, 3 * slots * points), jnp.bfloat16),
            vec,
        ),
        in_specs=[vmem] * 5,
        out_specs=(vmem,) * 3,
        name="prepare",
    )(w_flat, visibility, inverses, grad_points, cams_placed)

    got = lax.all_gather(send, ("row", "col"), axis=0, tiled=False)

    def product(known):
        return pl.pallas_call(
            functools.partial(product_kernel, slots, blocks, len(known)),
            out_shape=vec,
            in_specs=[smem] + [vmem] * (4 + len(known)),
            out_specs=vmem,
            name="product",
        )(place, visibility, w_flat, zw, cam_wide, *known)

    def reduce_all(value):
        return all_sum(value, blocks, n_row, n_col)

    rhs = reduce_all(part)
    known = [rhs]
    known.append(reduce_all(product(known)))
    got, known = lax.optimization_barrier((got, known))

    pair = 2
    tile = pl.pallas_call(
        functools.partial(tile_kernel, slots, blocks, width, strip),
        out_shape=jax.ShapeDtypeStruct((set_rows, col_count), jnp.float32),
        grid=(shards // pair,),
        in_specs=[
            smem,
            pl.BlockSpec((pair, send_rows, points), lambda i: (i, 0, 0)),
            pl.BlockSpec((strip, width), lambda i: (0, 0)),
        ],
        out_specs=pl.BlockSpec((set_rows, col_count), lambda i: (0, 0)),
        scratch_shapes=[
            pltpu.VMEM((set_rows, 3 * pair * points), jnp.bfloat16),
            pltpu.VMEM((col_count, 3 * pair * points), jnp.bfloat16),
        ],
        compiler_params=pltpu.CompilerParams(
            dimension_semantics=("arbitrary",), vmem_limit_bytes=40 * 1024 * 1024
        ),
        cost_estimate=pl.CostEstimate(
            flops=2 * set_rows * col_count * 3 * shards * points,
            bytes_accessed=2 * shards * send_rows * points + 4 * set_rows * col_count,
            transcendentals=0,
        ),
        name="tile",
    )(place, got, camera_blocks)

    tile, known = lax.optimization_barrier((tile, known))
    schur = lax.psum_scatter(tile, "pts", scatter_dimension=0, tiled=True)
    for _ in range(1, ITERS):
        known.append(reduce_all(product(known)))
    answer = pl.pallas_call(answer_kernel, out_shape=vec, in_specs=[vmem] * 4, out_specs=vmem, name="answer")(*known)

    def own(value):
        return lax.dynamic_slice(value, (pts_idx, row_idx * strip), (1, strip)).reshape(strip)

    return (schur, own(rhs), own(answer))


def solution(mesh):
    return jax.shard_map(
        per_device,
        mesh=mesh,
        in_specs=(
            P(None, ("pts", "row", "col"), None),
            P(None, ("pts", "row", "col")),
            P(None, ("pts", "row", "col")),
            P(None, ("pts", "row", "col")),
            P(("pts", "row"), None),
            P(("pts", "row")),
        ),
        out_specs=(P(("pts", "row"), "col"), P(("pts", "row")), P(("pts", "row"))),
        check_vma=False,
    )
```

```python
import functools

import jax
import jax.numpy as jnp
from jax import lax
from jax.experimental import pallas as pl
from jax.experimental.pallas import tpu as pltpu
from jax.sharding import Mesh
from jax.sharding import PartitionSpec as P

ITERS = 3
NT = (((1,), (1,)), ((), ()))
AUX = 16


def total(first, second):
    return jnp.sum(jnp.sum(first * second, axis=1, keepdims=True), axis=0, keepdims=True)


def minres(rhs_vec, products):
    beta_first = jnp.sqrt(total(rhs_vec, rhs_vec))
    r_older = rhs_vec
    r_old = rhs_vec
    lanczos = rhs_vec
    zero = jnp.zeros_like(beta_first)
    beta_old = zero
    beta_now = beta_first
    d_bar = zero
    eps_now = zero
    phi_bar = beta_first
    cos_now = zero - 1.0
    sin_now = zero
    w_now = jnp.zeros_like(rhs_vec)
    w_old = jnp.zeros_like(rhs_vec)
    answer = jnp.zeros_like(rhs_vec)
    for turn in range(ITERS):
        v_now = lanczos / beta_now
        if turn == len(products):
            return v_now
        lanczos = products[turn]
        if turn > 0:
            lanczos = lanczos - beta_now / beta_old * r_older
        alpha_now = total(v_now, lanczos)
        lanczos = lanczos - alpha_now / beta_now * r_old
        beta_old = beta_now
        beta_now = jnp.sqrt(total(lanczos, lanczos))
        r_older = r_old
        r_old = lanczos
        eps_old = eps_now
        delta_now = cos_now * d_bar + sin_now * alpha_now
        g_bar = sin_now * d_bar - cos_now * alpha_now
        eps_now = sin_now * beta_now
        d_bar = -cos_now * beta_now
        gamma_now = jnp.sqrt(g_bar * g_bar + beta_now * beta_now)
        cos_now = g_bar / gamma_now
        sin_now = beta_now / gamma_now
        phi_now = cos_now * phi_bar
        phi_bar = sin_now * phi_bar
        w_older = w_old
        w_old = w_now
        w_now = (v_now - eps_old * w_older - delta_now * w_old) / gamma_now
        answer = answer + phi_now * w_now
    return answer


def apply_inverse(inv, rows):
    return (
        inv[0] * rows[0] + inv[3] * rows[1] + inv[4] * rows[2],
        inv[3] * rows[0] + inv[1] * rows[1] + inv[5] * rows[2],
        inv[4] * rows[0] + inv[5] * rows[1] + inv[2] * rows[2],
    )


def slot_masks(vis, blocks):
    points = vis.shape[1]
    ids = lax.broadcasted_iota(jnp.int32, (blocks, points), 0)
    return [(vis[k : k + 1, :] == ids).astype(jnp.float32) for k in range(vis.shape[0])]


def prepare_kernel(slots, blocks, w_ref, vis_ref, inv_ref, grad_ref, cams_ref, send_ref, zw_ref, part_ref):
    points = vis_ref.shape[1]
    width = w_ref.shape[1]
    inv = inv_ref[...].astype(jnp.float32)
    inv_rows = [inv[e : e + 1, :] for e in range(6)]
    grad = grad_ref[...].astype(jnp.float32)
    vis = vis_ref[...]
    for k in range(slots):
        turned = []
        for a in range(3):
            at = 3 * k + a
            t = jnp.transpose(w_ref[at * points : (at + 1) * points, :].astype(jnp.float32))
            turned.append(t)
            send_ref[at * width : (at + 1) * width, :] = t.astype(jnp.bfloat16)
        for a, z in enumerate(apply_inverse(inv_rows, turned)):
            at = 3 * k + a
            zw_ref[:, at * points : (at + 1) * points] = z.astype(jnp.bfloat16)
    pad = jnp.zeros((AUX - slots - 6, points), jnp.float32)
    aux = jnp.concatenate([vis.astype(jnp.float32), inv, pad], axis=0)
    send_ref[3 * slots * width :, :] = aux.astype(jnp.bfloat16)
    masks = slot_masks(vis, blocks)
    moved = apply_inverse(inv_rows, [grad[a : a + 1, :] for a in range(3)])
    moved = [e.astype(jnp.bfloat16).astype(jnp.float32) for e in moved]
    lhs = jnp.concatenate([masks[k] * moved[a] for k in range(slots) for a in range(3)], axis=1)
    terms = jnp.dot(lhs.astype(jnp.bfloat16), w_ref[...], preferred_element_type=jnp.float32)
    part_ref[...] = cams_ref[...] - terms


def split(x):
    high = x.astype(jnp.bfloat16)
    low = (x - high.astype(jnp.float32)).astype(jnp.bfloat16)
    return high, low


def product_kernel(slots, blocks, n_known, *refs):
    place_ref, vis_ref, w_ref, zw_ref, cam_ref = refs[:5]
    known = refs[5 : 5 + n_known]
    out_ref = refs[5 + n_known]
    points = vis_ref.shape[1]
    v = minres(known[0][...], [r[...] for r in known[1:]])
    masks = slot_masks(vis_ref[...], blocks)
    v2 = jnp.concatenate(split(v), axis=0)
    dots = jnp.dot(v2, zw_ref[...], preferred_element_type=jnp.float32)
    dots = dots[:blocks] + dots[blocks:]
    t = []
    for a in range(3):
        s = None
        for k in range(slots):
            at = 3 * k + a
            term = masks[k] * dots[:, at * points : (at + 1) * points]
            s = term if s is None else s + term
        t.append(jnp.sum(s, axis=0, keepdims=True))
    lhs = jnp.concatenate([masks[k] * t[a] for k in range(slots) for a in range(3)], axis=1)
    lhs2 = jnp.concatenate(split(lhs), axis=0)
    terms = jnp.dot(lhs2, w_ref[...], preferred_element_type=jnp.float32)
    rows = lax.broadcasted_iota(jnp.int32, v.shape, 0)
    own = jnp.where(rows == 2 * place_ref[0] + place_ref[1], v, 0.0)
    cams = jnp.dot(own, cam_ref[...], precision=lax.Precision.HIGHEST, preferred_element_type=jnp.float32)
    out_ref[...] = cams - terms[:blocks] - terms[blocks:]


def answer_kernel(rhs_ref, s1_ref, s2_ref, s3_ref, out_ref):
    out_ref[...] = minres(rhs_ref[...], [s1_ref[...], s2_ref[...], s3_ref[...]])


def chosen(picks, terms):
    value = None
    for pick, term in zip(picks, terms):
        part = pick * term
        value = part if value is None else value + part
    return value


def tile_kernel(slots, blocks, width, strip, fine, place_ref, got_ref, cam_ref, own_ref, peer_ref, acc_ref, row_ref, col_ref):
    z_idx, core_idx, row_idx, col_idx = place_ref[0], place_ref[1], place_ref[2], place_ref[3]
    sources, _, points = got_ref.shape
    half, col_count = own_ref.shape
    col_blocks = col_count // width
    base_aux = 3 * slots * width

    @pl.when(pl.program_id(0) == 0)
    def _():
        own_ref[...] = jnp.zeros_like(own_ref)
        acc_ref[...] = jnp.zeros_like(acc_ref)
        for c in range(col_blocks):

            @pl.when(col_idx * col_blocks + c == 2 * z_idx + core_idx)
            def _():
                start = pl.multiple_of(z_idx * strip, strip)
                own_ref[pl.ds(start, strip), c * width : (c + 1) * width] = cam_ref[...]

    for s in range(sources):
        aux = got_ref[s, base_aux : base_aux + AUX, :].astype(jnp.float32)
        vis = [aux[k : k + 1, :] for k in range(slots)]
        inv = [aux[slots + e : slots + e + 1, :] for e in range(6)]

        def picks_of(block, one):
            block = block.astype(jnp.float32)
            return [jnp.where(v == block, one, 0.0).astype(jnp.bfloat16) for v in vis]

        col_picks = [picks_of(col_idx * col_blocks + c, 1.0) for c in range(col_blocks)]

        @pl.loop(0, width // fine)
        def _(h):
            terms = []
            for at in range(3 * slots):
                start = pl.multiple_of(at * width + h * fine, fine)
                terms.append(got_ref[s, pl.ds(start, fine), :])
            for c in range(col_blocks):
                rows = [chosen(col_picks[c], terms[a::3]).astype(jnp.float32) for a in range(3)]
                start = pl.multiple_of(c * width + h * fine, fine)
                for a, z in enumerate(apply_inverse(inv, rows)):
                    at = (a * sources + s) * points
                    col_ref[pl.ds(start, fine), at : at + points] = z.astype(jnp.bfloat16)

        @pl.loop(0, strip // fine)
        def _(h):
            terms = []
            for at in range(3 * slots):
                start = pl.multiple_of(at * width + row_idx * strip + h * fine, fine)
                terms.append(got_ref[s, pl.ds(start, fine), :])
            for b in range(blocks):
                other = b >= blocks // 2
                picks = picks_of(2 * (b % (blocks // 2)) + (1 - core_idx if other else core_idx), -1.0)
                start = pl.multiple_of(b * strip + h * fine, fine)
                for a in range(3):
                    at = (a * sources + s) * points
                    row_ref[pl.ds(start, fine), at : at + points] = chosen(picks, terms[a::3])

    acc_ref[...] += lax.dot_general(row_ref[half:, :], col_ref[...], NT, preferred_element_type=jnp.float32)
    own_ref[...] += lax.dot_general(row_ref[:half, :], col_ref[...], NT, preferred_element_type=jnp.float32)

    @pl.when(pl.program_id(0) == pl.num_programs(0) - 1)
    def _():
        peer_ref[...] = acc_ref[...].astype(jnp.bfloat16)


def tree(values):
    while len(values) > 1:
        values = [values[i] + values[i + 1] for i in range(0, len(values), 2)]
    return values[0]


def core_sum(value):
    return value + lax.ppermute(value, "core", [(0, 1), (1, 0)])


def all_sum(value, n_z, n_row, n_col):
    value = core_sum(value)
    far = n_z // 2
    pairs = [[(2 * z + c, 2 * (z ^ (j + c * far)) + c) for z in range(n_z) for c in range(2)] for j in range(far)]
    value = tree([lax.ppermute(value, ("z", "core"), p) for p in pairs])
    for axis, size in (("row", n_row), ("col", n_col)):
        swaps = [lax.ppermute(value, axis, [(i, i ^ b) for i in range(size)]) for b in range(1, size)]
        value = tree([value] + swaps)
    return core_sum(value)


def per_device(weights, visibility, inverses, grad_points, camera_blocks, grad_cams):
    n_row = lax.axis_size("row")
    n_col = lax.axis_size("col")
    n_z = lax.axis_size("z")
    blocks = 2 * n_z
    z_idx = lax.axis_index("z")
    core_idx = lax.axis_index("core")
    pts_idx = 2 * z_idx + core_idx
    row_idx = lax.axis_index("row")
    col_idx = lax.axis_index("col")
    slots, points = visibility.shape
    width = weights.shape[2]
    strip = width // n_row
    total_rows = blocks * width
    col_count = total_rows // n_col
    set_rows = blocks * strip
    shards = n_row * n_col
    send_rows = 3 * slots * width + AUX
    place = jnp.stack([z_idx, core_idx, row_idx, col_idx]).astype(jnp.int32)
    w_flat = weights.reshape(3 * slots * points, width)
    first_col = (col_idx == 0).astype(jnp.float32)
    lanes = jnp.arange(width, dtype=jnp.int32)[None, :]
    own_lanes = (lanes // strip == row_idx) & (jnp.arange(blocks, dtype=jnp.int32)[:, None] == pts_idx)
    cams_placed = jnp.where(own_lanes, jnp.tile(grad_cams, n_row)[None, :] * first_col, 0.0)
    cam_wide = lax.dynamic_update_slice(
        jnp.zeros((width, width), jnp.float32), camera_blocks * first_col, (row_idx * strip, 0)
    )
    vmem = pl.BlockSpec(memory_space=pltpu.VMEM)
    smem = pl.BlockSpec(memory_space=pltpu.SMEM)
    vec = jax.ShapeDtypeStruct((blocks, width), jnp.float32)

    send, zw, part = pl.pallas_call(
        functools.partial(prepare_kernel, slots, blocks),
        out_shape=(
            jax.ShapeDtypeStruct((send_rows, points), jnp.bfloat16),
            jax.ShapeDtypeStruct((width, 3 * slots * points), jnp.bfloat16),
            vec,
        ),
        in_specs=[vmem] * 5,
        out_specs=(vmem,) * 3,
        name="prepare",
    )(w_flat, visibility, inverses, grad_points, cams_placed)

    got = lax.all_gather(send, ("row", "col"), axis=0, tiled=False)

    def product(known):
        return pl.pallas_call(
            functools.partial(product_kernel, slots, blocks, len(known)),
            out_shape=vec,
            in_specs=[smem] + [vmem] * (4 + len(known)),
            out_specs=vmem,
            name="product",
        )(place, visibility, w_flat, zw, cam_wide, *known)

    def reduce_all(value):
        return all_sum(value, n_z, n_row, n_col)

    rhs = reduce_all(part)
    known = [rhs]
    for _ in range(1, ITERS):
        known.append(reduce_all(product(known)))
    got, known = lax.optimization_barrier((got, known))

    pair = 2
    half = set_rows // 2
    own_half, peer_half = pl.pallas_call(
        functools.partial(tile_kernel, slots, blocks, width, strip, 64),
        out_shape=(
            jax.ShapeDtypeStruct((half, col_count), jnp.float32),
            jax.ShapeDtypeStruct((half, col_count), jnp.bfloat16),
        ),
        grid=(shards // pair,),
        in_specs=[
            smem,
            pl.BlockSpec((pair, send_rows, points), lambda i: (i, 0, 0)),
            pl.BlockSpec((strip, width), lambda i: (0, 0)),
        ],
        out_specs=(
            pl.BlockSpec((half, col_count), lambda i: (0, 0)),
            pl.BlockSpec((half, col_count), lambda i: (0, 0)),
        ),
        scratch_shapes=[
            pltpu.VMEM((half, col_count), jnp.float32),
            pltpu.VMEM((set_rows, 3 * pair * points), jnp.bfloat16),
            pltpu.VMEM((col_count, 3 * pair * points), jnp.bfloat16),
        ],
        compiler_params=pltpu.CompilerParams(
            dimension_semantics=("arbitrary",), vmem_limit_bytes=56 * 1024 * 1024
        ),
        cost_estimate=pl.CostEstimate(
            flops=2 * set_rows * col_count * 3 * shards * points,
            bytes_accessed=2 * shards * send_rows * points + 4 * set_rows * col_count,
            transcendentals=0,
        ),
        name="tile",
    )(place, got, camera_blocks)
    taken = lax.ppermute(peer_half, "core", [(0, 1), (1, 0)])
    tile = own_half + taken.astype(jnp.float32)
    tile, known = lax.optimization_barrier((tile, known))
    schur = lax.psum_scatter(tile, "z", scatter_dimension=0, tiled=True)
    known.append(reduce_all(product(known)))
    answer = pl.pallas_call(answer_kernel, out_shape=vec, in_specs=[vmem] * 4, out_specs=vmem, name="answer")(*known)

    def own(value):
        return lax.dynamic_slice(value, (pts_idx, row_idx * strip), (1, strip)).reshape(strip)

    return (schur, own(rhs), own(answer))


def solution(mesh):
    n_pts, n_row, n_col = (mesh.shape[axis] for axis in ("pts", "row", "col"))
    cores = Mesh(mesh.devices.reshape(n_pts // 2, 2, n_row, n_col), ("z", "core", "row", "col"))
    pts = ("z", "core")
    return jax.shard_map(
        per_device,
        mesh=cores,
        in_specs=(
            P(None, (*pts, "row", "col"), None),
            P(None, (*pts, "row", "col")),
            P(None, (*pts, "row", "col")),
            P(None, (*pts, "row", "col")),
            P((*pts, "row"), None),
            P((*pts, "row")),
        ),
        out_specs=(P((*pts, "row"), "col"), P((*pts, "row")), P((*pts, "row"))),
        check_vma=False,
    )
```

```python
import functools

import jax
import jax.numpy as jnp
from jax import lax
from jax.experimental import pallas as pl
from jax.experimental.pallas import tpu as pltpu
from jax.sharding import Mesh
from jax.sharding import PartitionSpec as P

ITERS = 3
NT = (((1,), (1,)), ((), ()))
AUX = 16


def total(first, second):
    return jnp.sum(jnp.sum(first * second, axis=1, keepdims=True), axis=0, keepdims=True)


def minres(rhs_vec, products):
    beta_first = jnp.sqrt(total(rhs_vec, rhs_vec))
    r_older = rhs_vec
    r_old = rhs_vec
    lanczos = rhs_vec
    zero = jnp.zeros_like(beta_first)
    beta_old = zero
    beta_now = beta_first
    d_bar = zero
    eps_now = zero
    phi_bar = beta_first
    cos_now = zero - 1.0
    sin_now = zero
    w_now = jnp.zeros_like(rhs_vec)
    w_old = jnp.zeros_like(rhs_vec)
    answer = jnp.zeros_like(rhs_vec)
    for turn in range(ITERS):
        v_now = lanczos / beta_now
        if turn == len(products):
            return v_now
        lanczos = products[turn]
        if turn > 0:
            lanczos = lanczos - beta_now / beta_old * r_older
        alpha_now = total(v_now, lanczos)
        lanczos = lanczos - alpha_now / beta_now * r_old
        beta_old = beta_now
        beta_now = jnp.sqrt(total(lanczos, lanczos))
        r_older = r_old
        r_old = lanczos
        eps_old = eps_now
        delta_now = cos_now * d_bar + sin_now * alpha_now
        g_bar = sin_now * d_bar - cos_now * alpha_now
        eps_now = sin_now * beta_now
        d_bar = -cos_now * beta_now
        gamma_now = jnp.sqrt(g_bar * g_bar + beta_now * beta_now)
        cos_now = g_bar / gamma_now
        sin_now = beta_now / gamma_now
        phi_now = cos_now * phi_bar
        phi_bar = sin_now * phi_bar
        w_older = w_old
        w_old = w_now
        w_now = (v_now - eps_old * w_older - delta_now * w_old) / gamma_now
        answer = answer + phi_now * w_now
    return answer


def apply_inverse(inv, rows):
    return (
        inv[0] * rows[0] + inv[3] * rows[1] + inv[4] * rows[2],
        inv[3] * rows[0] + inv[1] * rows[1] + inv[5] * rows[2],
        inv[4] * rows[0] + inv[5] * rows[1] + inv[2] * rows[2],
    )


def slot_masks(vis, blocks):
    points = vis.shape[1]
    ids = lax.broadcasted_iota(jnp.int32, (blocks, points), 0)
    return [(vis[k : k + 1, :] == ids).astype(jnp.float32) for k in range(vis.shape[0])]


def prepare_kernel(slots, blocks, w_ref, vis_ref, inv_ref, grad_ref, cams_ref, send_ref, zw_ref, part_ref):
    points = vis_ref.shape[1]
    width = w_ref.shape[1]
    inv = inv_ref[...].astype(jnp.float32)
    inv_rows = [inv[e : e + 1, :] for e in range(6)]
    grad = grad_ref[...].astype(jnp.float32)
    vis = vis_ref[...]
    for k in range(slots):
        turned = []
        for a in range(3):
            at = 3 * k + a
            t = jnp.transpose(w_ref[at * points : (at + 1) * points, :].astype(jnp.float32))
            turned.append(t)
            send_ref[at * width : (at + 1) * width, :] = t.astype(jnp.bfloat16)
        for a, z in enumerate(apply_inverse(inv_rows, turned)):
            at = 3 * k + a
            zw_ref[:, at * points : (at + 1) * points] = z.astype(jnp.bfloat16)
    pad = jnp.zeros((AUX - slots - 6, points), jnp.float32)
    aux = jnp.concatenate([vis.astype(jnp.float32), inv, pad], axis=0)
    send_ref[3 * slots * width :, :] = aux.astype(jnp.bfloat16)
    masks = slot_masks(vis, blocks)
    moved = apply_inverse(inv_rows, [grad[a : a + 1, :] for a in range(3)])
    moved = [e.astype(jnp.bfloat16).astype(jnp.float32) for e in moved]
    lhs = jnp.concatenate([masks[k] * moved[a] for k in range(slots) for a in range(3)], axis=1)
    terms = jnp.dot(lhs.astype(jnp.bfloat16), w_ref[...], preferred_element_type=jnp.float32)
    part_ref[...] = cams_ref[...] - terms


def split(x):
    high = x.astype(jnp.bfloat16)
    low = (x - high.astype(jnp.float32)).astype(jnp.bfloat16)
    return high, low


def product_kernel(slots, blocks, n_known, *refs):
    place_ref, vis_ref, w_ref, zw_ref, cam_ref = refs[:5]
    known = refs[5 : 5 + n_known]
    out_ref = refs[5 + n_known]
    points = vis_ref.shape[1]
    v = minres(known[0][...], [r[...] for r in known[1:]])
    masks = slot_masks(vis_ref[...], blocks)
    v2 = jnp.concatenate(split(v), axis=0)
    dots = jnp.dot(v2, zw_ref[...], preferred_element_type=jnp.float32)
    dots = dots[:blocks] + dots[blocks:]
    t = []
    for a in range(3):
        s = None
        for k in range(slots):
            at = 3 * k + a
            term = masks[k] * dots[:, at * points : (at + 1) * points]
            s = term if s is None else s + term
        t.append(jnp.sum(s, axis=0, keepdims=True))
    lhs = jnp.concatenate([masks[k] * t[a] for k in range(slots) for a in range(3)], axis=1)
    lhs2 = jnp.concatenate(split(lhs), axis=0)
    terms = jnp.dot(lhs2, w_ref[...], preferred_element_type=jnp.float32)
    rows = lax.broadcasted_iota(jnp.int32, v.shape, 0)
    own = jnp.where(rows == 2 * place_ref[0] + place_ref[1], v, 0.0)
    cams = jnp.dot(own, cam_ref[...], precision=lax.Precision.HIGHEST, preferred_element_type=jnp.float32)
    out_ref[...] = cams - terms[:blocks] - terms[blocks:]


def answer_kernel(strip, place_ref, rhs_ref, s1_ref, s2_ref, s3_ref, own_rhs_ref, own_ref):
    rhs = rhs_ref[...]
    answer = minres(rhs, [s1_ref[...], s2_ref[...], s3_ref[...]])
    rows = lax.broadcasted_iota(jnp.int32, rhs.shape, 0)
    for value, ref in ((rhs, own_rhs_ref), (answer, own_ref)):
        line = jnp.sum(jnp.where(rows == 2 * place_ref[0] + place_ref[1], value, 0.0), axis=0, keepdims=True)
        for r in range(rhs.shape[1] // strip):

            @pl.when(place_ref[2] == r)
            def _():
                ref[...] = line[:, r * strip : (r + 1) * strip]


def chosen(picks, terms):
    value = None
    for pick, term in zip(picks, terms):
        part = pick * term
        value = part if value is None else value + part
    return value


def tile_kernel(slots, blocks, width, strip, fine, offsets, place_ref, got_ref, cam_ref, *refs):
    count = len(offsets)
    out_refs, (acc_ref, row_ref, col_ref) = refs[:count], refs[count:]
    z_idx, core_idx, row_idx, col_idx = place_ref[0], place_ref[1], place_ref[2], place_ref[3]
    sources, _, points = got_ref.shape
    col_count = acc_ref.shape[2]
    col_blocks = col_count // width
    base_aux = 3 * slots * width

    @pl.when(pl.program_id(0) == 0)
    def _():
        acc_ref[...] = jnp.zeros_like(acc_ref)
        if offsets[0] == 0:
            for c in range(col_blocks):

                @pl.when(col_idx * col_blocks + c == 2 * z_idx + core_idx)
                def _():
                    start = pl.multiple_of(z_idx * strip, strip)
                    acc_ref[0, pl.ds(start, strip), c * width : (c + 1) * width] = cam_ref[...]

    @pl.loop(0, sources)
    def _(s):
        aux = got_ref[s, base_aux : base_aux + AUX, :].astype(jnp.float32)
        vis = [aux[k : k + 1, :] for k in range(slots)]
        inv = [aux[slots + e : slots + e + 1, :] for e in range(6)]

        def picks_of(block, one):
            block = block.astype(jnp.float32)
            return [jnp.where(v == block, one, 0.0).astype(jnp.bfloat16) for v in vis]

        @pl.loop(0, count)
        def _(d):
            first = (col_idx ^ (d + offsets[0])) * col_blocks
            col_picks = [picks_of(first + c, 1.0) for c in range(col_blocks)]

            @pl.loop(0, width // fine)
            def _(h):
                terms = []
                for at in range(3 * slots):
                    start = pl.multiple_of(at * width + h * fine, fine)
                    terms.append(got_ref[s, pl.ds(start, fine), :])
                for c in range(col_blocks):
                    rows = [chosen(col_picks[c], terms[a::3]).astype(jnp.float32) for a in range(3)]
                    start = pl.multiple_of(c * width + h * fine, fine)
                    for a, z in enumerate(apply_inverse(inv, rows)):
                        at = pl.multiple_of((a * sources + s) * points, points)
                        col_ref[d, pl.ds(start, fine), pl.ds(at, points)] = z.astype(jnp.bfloat16)

        @pl.loop(0, strip // fine)
        def _(h):
            terms = []
            for at in range(3 * slots):
                start = pl.multiple_of(at * width + row_idx * strip + h * fine, fine)
                terms.append(got_ref[s, pl.ds(start, fine), :])
            for b in range(blocks // 2):
                picks = picks_of(2 * b + core_idx, -1.0)
                start = pl.multiple_of(b * strip + h * fine, fine)
                for a in range(3):
                    at = pl.multiple_of((a * sources + s) * points, points)
                    row_ref[pl.ds(start, fine), pl.ds(at, points)] = chosen(picks, terms[a::3])

    @pl.loop(0, count)
    def _(d):
        acc_ref[d] += lax.dot_general(row_ref[...], col_ref[d], NT, preferred_element_type=jnp.float32)

    @pl.when(pl.program_id(0) == pl.num_programs(0) - 1)
    def _():
        for d in range(count):
            out_refs[d][...] = acc_ref[d].astype(out_refs[d].dtype)


def tree(values):
    while len(values) > 1:
        values = [values[i] + values[i + 1] for i in range(0, len(values), 2)]
    return values[0]


def core_sum(value):
    return value + lax.ppermute(value, "core", [(0, 1), (1, 0)])


def all_sum(value, n_z, n_row, n_col, between=None):
    value = core_sum(value)
    far = n_z // 2
    pairs = [[(2 * z + c, 2 * (z ^ (j + c * far)) + c) for z in range(n_z) for c in range(2)] for j in range(far)]
    value = tree([lax.ppermute(value, ("z", "core"), p) for p in pairs])
    if between is not None:
        value = between(value)
    for axis, size in (("row", n_row), ("col", n_col)):
        swaps = [lax.ppermute(value, axis, [(i, i ^ b) for i in range(size)]) for b in range(1, size)]
        value = tree([value] + swaps)
    return core_sum(value)


def per_device(weights, visibility, inverses, grad_points, camera_blocks, grad_cams):
    n_row = lax.axis_size("row")
    n_col = lax.axis_size("col")
    n_z = lax.axis_size("z")
    blocks = 2 * n_z
    z_idx = lax.axis_index("z")
    core_idx = lax.axis_index("core")
    pts_idx = 2 * z_idx + core_idx
    row_idx = lax.axis_index("row")
    col_idx = lax.axis_index("col")
    slots, points = visibility.shape
    width = weights.shape[2]
    strip = width // n_row
    total_rows = blocks * width
    col_count = total_rows // n_col
    set_rows = blocks * strip
    shards = 2 * n_row
    send_rows = 3 * slots * width + AUX
    place = jnp.stack([z_idx, core_idx, row_idx, col_idx]).astype(jnp.int32)
    w_flat = weights.reshape(3 * slots * points, width)
    first_col = (col_idx == 0).astype(jnp.float32)
    lanes = jnp.arange(width, dtype=jnp.int32)[None, :]
    own_lanes = (lanes // strip == row_idx) & (jnp.arange(blocks, dtype=jnp.int32)[:, None] == pts_idx)
    cams_placed = jnp.where(own_lanes, jnp.tile(grad_cams, n_row)[None, :] * first_col, 0.0)
    cam_wide = lax.dynamic_update_slice(
        jnp.zeros((width, width), jnp.float32), camera_blocks * first_col, (row_idx * strip, 0)
    )
    vmem = pl.BlockSpec(memory_space=pltpu.VMEM)
    smem = pl.BlockSpec(memory_space=pltpu.SMEM)
    vec = jax.ShapeDtypeStruct((blocks, width), jnp.float32)

    send, zw, part = pl.pallas_call(
        functools.partial(prepare_kernel, slots, blocks),
        out_shape=(
            jax.ShapeDtypeStruct((send_rows, points), jnp.bfloat16),
            jax.ShapeDtypeStruct((width, 3 * slots * points), jnp.bfloat16),
            vec,
        ),
        in_specs=[vmem] * 5,
        out_specs=(vmem,) * 3,
        name="prepare",
    )(w_flat, visibility, inverses, grad_points, cams_placed)

    got = lax.all_gather(send, ("core", "row"), axis=0, tiled=False)

    def product(known):
        return pl.pallas_call(
            functools.partial(product_kernel, slots, blocks, len(known)),
            out_shape=vec,
            in_specs=[smem] + [vmem] * (4 + len(known)),
            out_specs=vmem,
            name="product",
        )(place, visibility, w_flat, zw, cam_wide, *known)

    pair = 2
    half = set_rows // 2

    def pieces_of(got, offsets, dtype):
        return pl.pallas_call(
            functools.partial(tile_kernel, slots, blocks, width, strip, 64, offsets),
            out_shape=(jax.ShapeDtypeStruct((half, col_count), dtype),) * len(offsets),
            grid=(shards // pair,),
            in_specs=[
                smem,
                pl.BlockSpec((pair, send_rows, points), lambda i: (i, 0, 0)),
                pl.BlockSpec((strip, width), lambda i: (0, 0)),
            ],
            out_specs=(pl.BlockSpec((half, col_count), lambda i: (0, 0)),) * len(offsets),
            scratch_shapes=[
                pltpu.VMEM((len(offsets), half, col_count), jnp.float32),
                pltpu.VMEM((half, 3 * pair * points), jnp.bfloat16),
                pltpu.VMEM((len(offsets), col_count, 3 * pair * points), jnp.bfloat16),
            ],
            compiler_params=pltpu.CompilerParams(
                dimension_semantics=("arbitrary",), vmem_limit_bytes=56 * 1024 * 1024
            ),
            cost_estimate=pl.CostEstimate(
                flops=2 * len(offsets) * half * col_count * 3 * shards * points,
                bytes_accessed=2 * shards * send_rows * points + 4 * len(offsets) * half * col_count,
                transcendentals=0,
            ),
            name="tile",
        )(place, got, camera_blocks)

    held = {}

    def make_tile(value):
        here, value = lax.optimization_barrier((got, value))
        offsets = tuple(range(1, n_col))
        pieces, value = lax.optimization_barrier((pieces_of(here, offsets, jnp.bfloat16), value))
        held["taken"] = [
            lax.ppermute(piece, "col", [(i, i ^ offset) for i in range(n_col)]) for piece, offset in zip(pieces, offsets)
        ]
        (held["own"],), value = lax.optimization_barrier((pieces_of(here, (0,), jnp.float32), value))
        return value

    def reduce_tile(value):
        tile = tree([held["own"]] + [piece.astype(jnp.float32) for piece in held["taken"]])
        tile, value = lax.optimization_barrier((tile, value))
        held["schur"] = lax.psum_scatter(tile, "z", scatter_dimension=0, tiled=True)
        return value

    known = [all_sum(part, n_z, n_row, n_col)]
    for between in (make_tile, reduce_tile, None):
        known.append(all_sum(product(known), n_z, n_row, n_col, between))
    own = jax.ShapeDtypeStruct((1, strip), jnp.float32)
    own_rhs, answer = pl.pallas_call(
        functools.partial(answer_kernel, strip),
        out_shape=(own, own),
        in_specs=[smem] + [vmem] * 4,
        out_specs=(vmem, vmem),
        name="answer",
    )(place, *known)
    return (held["schur"], own_rhs.reshape(strip), answer.reshape(strip))


def solution(mesh):
    n_pts, n_row, n_col = (mesh.shape[axis] for axis in ("pts", "row", "col"))
    cores = Mesh(mesh.devices.reshape(n_pts // 2, 2, n_row, n_col), ("z", "core", "row", "col"))
    pts = ("z", "core")
    return jax.shard_map(
        per_device,
        mesh=cores,
        in_specs=(
            P(None, (*pts, "row", "col"), None),
            P(None, (*pts, "row", "col")),
            P(None, (*pts, "row", "col")),
            P(None, (*pts, "row", "col")),
            P((*pts, "row"), None),
            P((*pts, "row")),
        ),
        out_specs=(P((*pts, "row"), "col"), P((*pts, "row")), P((*pts, "row"))),
        check_vma=False,
    )
```

```python
import functools

import jax
import jax.numpy as jnp
from jax import lax
from jax.experimental import pallas as pl
from jax.experimental.pallas import tpu as pltpu
from jax.sharding import Mesh
from jax.sharding import PartitionSpec as P

ITERS = 3
NT = (((1,), (1,)), ((), ()))
AUX = 16


def total(first, second):
    return jnp.sum(jnp.sum(first * second, axis=1, keepdims=True), axis=0, keepdims=True)


def minres(rhs_vec, products):
    beta_first = jnp.sqrt(total(rhs_vec, rhs_vec))
    r_older = rhs_vec
    r_old = rhs_vec
    lanczos = rhs_vec
    zero = jnp.zeros_like(beta_first)
    beta_old = zero
    beta_now = beta_first
    d_bar = zero
    eps_now = zero
    phi_bar = beta_first
    cos_now = zero - 1.0
    sin_now = zero
    w_now = jnp.zeros_like(rhs_vec)
    w_old = jnp.zeros_like(rhs_vec)
    answer = jnp.zeros_like(rhs_vec)
    for turn in range(ITERS):
        v_now = lanczos / beta_now
        if turn == len(products):
            return v_now
        lanczos = products[turn]
        if turn > 0:
            lanczos = lanczos - beta_now / beta_old * r_older
        alpha_now = total(v_now, lanczos)
        lanczos = lanczos - alpha_now / beta_now * r_old
        beta_old = beta_now
        beta_now = jnp.sqrt(total(lanczos, lanczos))
        r_older = r_old
        r_old = lanczos
        eps_old = eps_now
        delta_now = cos_now * d_bar + sin_now * alpha_now
        g_bar = sin_now * d_bar - cos_now * alpha_now
        eps_now = sin_now * beta_now
        d_bar = -cos_now * beta_now
        gamma_now = jnp.sqrt(g_bar * g_bar + beta_now * beta_now)
        cos_now = g_bar / gamma_now
        sin_now = beta_now / gamma_now
        phi_now = cos_now * phi_bar
        phi_bar = sin_now * phi_bar
        w_older = w_old
        w_old = w_now
        w_now = (v_now - eps_old * w_older - delta_now * w_old) / gamma_now
        answer = answer + phi_now * w_now
    return answer


def apply_inverse(inv, rows):
    return (
        inv[0] * rows[0] + inv[3] * rows[1] + inv[4] * rows[2],
        inv[3] * rows[0] + inv[1] * rows[1] + inv[5] * rows[2],
        inv[4] * rows[0] + inv[5] * rows[1] + inv[2] * rows[2],
    )


def slot_masks(vis, blocks):
    points = vis.shape[1]
    ids = lax.broadcasted_iota(jnp.int32, (blocks, points), 0)
    return [(vis[k : k + 1, :] == ids).astype(jnp.float32) for k in range(vis.shape[0])]


def prepare_kernel(slots, blocks, w_ref, vis_ref, inv_ref, grad_ref, cams_ref, send_ref, zw_ref, part_ref):
    points = vis_ref.shape[1]
    width = w_ref.shape[1]
    inv = inv_ref[...].astype(jnp.float32)
    inv_rows = [inv[e : e + 1, :] for e in range(6)]
    grad = grad_ref[...].astype(jnp.float32)
    vis = vis_ref[...]
    for k in range(slots):
        turned = []
        for a in range(3):
            at = 3 * k + a
            t = jnp.transpose(w_ref[at * points : (at + 1) * points, :].astype(jnp.float32))
            turned.append(t)
            send_ref[at * width : (at + 1) * width, :] = t.astype(jnp.bfloat16)
        for a, z in enumerate(apply_inverse(inv_rows, turned)):
            at = 3 * k + a
            zw_ref[:, at * points : (at + 1) * points] = z.astype(jnp.bfloat16)
    pad = jnp.zeros((AUX - slots - 6, points), jnp.float32)
    aux = jnp.concatenate([vis.astype(jnp.float32), inv, pad], axis=0)
    send_ref[3 * slots * width :, :] = aux.astype(jnp.bfloat16)
    masks = slot_masks(vis, blocks)
    moved = apply_inverse(inv_rows, [grad[a : a + 1, :] for a in range(3)])
    moved = [e.astype(jnp.bfloat16).astype(jnp.float32) for e in moved]
    lhs = jnp.concatenate([masks[k] * moved[a] for k in range(slots) for a in range(3)], axis=1)
    terms = jnp.dot(lhs.astype(jnp.bfloat16), w_ref[...], preferred_element_type=jnp.float32)
    part_ref[...] = cams_ref[...] - terms


def split(x):
    high = x.astype(jnp.bfloat16)
    low = (x - high.astype(jnp.float32)).astype(jnp.bfloat16)
    return high, low


def product_kernel(slots, blocks, n_known, *refs):
    place_ref, vis_ref, w_ref, zw_ref, cam_ref = refs[:5]
    known = refs[5 : 5 + n_known]
    out_ref = refs[5 + n_known]
    points = vis_ref.shape[1]
    v = minres(known[0][...], [r[...] for r in known[1:]])
    masks = slot_masks(vis_ref[...], blocks)
    v2 = jnp.concatenate(split(v), axis=0)
    dots = jnp.dot(v2, zw_ref[...], preferred_element_type=jnp.float32)
    dots = dots[:blocks] + dots[blocks:]
    t = []
    for a in range(3):
        s = None
        for k in range(slots):
            at = 3 * k + a
            term = masks[k] * dots[:, at * points : (at + 1) * points]
            s = term if s is None else s + term
        t.append(jnp.sum(s, axis=0, keepdims=True))
    lhs = jnp.concatenate([masks[k] * t[a] for k in range(slots) for a in range(3)], axis=1)
    lhs2 = jnp.concatenate(split(lhs), axis=0)
    terms = jnp.dot(lhs2, w_ref[...], preferred_element_type=jnp.float32)
    rows = lax.broadcasted_iota(jnp.int32, v.shape, 0)
    own = jnp.where(rows == 2 * place_ref[0] + place_ref[1], v, 0.0)
    cams = jnp.dot(own, cam_ref[...], precision=lax.Precision.HIGHEST, preferred_element_type=jnp.float32)
    out_ref[...] = cams - terms[:blocks] - terms[blocks:]


def answer_kernel(strip, place_ref, rhs_ref, s1_ref, s2_ref, s3_ref, own_rhs_ref, own_ref):
    rhs = rhs_ref[...]
    answer = minres(rhs, [s1_ref[...], s2_ref[...], s3_ref[...]])
    rows = lax.broadcasted_iota(jnp.int32, rhs.shape, 0)
    for value, ref in ((rhs, own_rhs_ref), (answer, own_ref)):
        line = jnp.sum(jnp.where(rows == 2 * place_ref[0] + place_ref[1], value, 0.0), axis=0, keepdims=True)
        for r in range(rhs.shape[1] // strip):

            @pl.when(place_ref[2] == r)
            def _():
                ref[...] = line[:, r * strip : (r + 1) * strip]


def chosen(picks, terms):
    value = None
    for pick, term in zip(picks, terms):
        part = pick * term
        value = part if value is None else value + part
    return value


def tile_kernel(slots, blocks, width, strip, parts, place_ref, got_ref, cam_ref, own_ref, peer_ref, acc_ref, *operands):
    z_idx, core_idx, row_idx, col_idx = place_ref[0], place_ref[1], place_ref[2], place_ref[3]
    sources, _, points = got_ref.shape
    half, col_count = own_ref.shape
    col_blocks = col_count // width
    base_aux = 3 * slots * width
    fine = 64
    step = pl.program_id(0)

    @pl.when(step == 0)
    def _():
        own_ref[...] = jnp.zeros_like(own_ref)
        acc_ref[...] = jnp.zeros_like(acc_ref)
        for c in range(col_blocks):

            @pl.when(col_idx * col_blocks + c == 2 * z_idx + core_idx)
            def _():
                start = pl.multiple_of(z_idx * strip, strip)
                own_ref[pl.ds(start, strip), c * width : (c + 1) * width] = cam_ref[...]

    def build(part, row_ref, col_ref):
        for s in range(sources):
            aux = got_ref[s, base_aux : base_aux + AUX, :].astype(jnp.float32)
            vis = [aux[k : k + 1, :] for k in range(slots)]
            inv = [aux[slots + e : slots + e + 1, :] for e in range(6)]

            def picks_of(block, one):
                block = block.astype(jnp.float32)
                return [jnp.where(v == block, one, 0.0).astype(jnp.bfloat16) for v in vis]

            col_picks = [picks_of(col_idx * col_blocks + c, 1.0) for c in range(col_blocks)]
            for h in range(0, width // parts, fine):
                terms = []
                for at in range(3 * slots):
                    start = pl.multiple_of(at * width + part * (width // parts) + h, fine)
                    terms.append(got_ref[s, pl.ds(start, fine), :])
                for c in range(col_blocks):
                    rows = [chosen(col_picks[c], terms[a::3]).astype(jnp.float32) for a in range(3)]
                    start = pl.multiple_of(c * width + part * (width // parts) + h, fine)
                    for a, z in enumerate(apply_inverse(inv, rows)):
                        at = (a * sources + s) * points
                        col_ref[pl.ds(start, fine), at : at + points] = z.astype(jnp.bfloat16)
            deep = strip // parts
            terms = []
            for at in range(3 * slots):
                start = pl.multiple_of(at * width + row_idx * strip + part * deep, deep)
                terms.append(got_ref[s, pl.ds(start, deep), :])
            for b in range(blocks):
                other = b >= blocks // 2
                picks = picks_of(2 * (b % (blocks // 2)) + (1 - core_idx if other else core_idx), -1.0)
                start = pl.multiple_of(b * strip + part * deep, deep)
                for a in range(3):
                    at = (a * sources + s) * points
                    row_ref[pl.ds(start, deep), at : at + points] = chosen(picks, terms[a::3])

    def multiply(part, row_ref, col_ref):
        span = col_count // parts
        cols = pl.ds(pl.multiple_of(part * span, span), span)
        terms = lax.dot_general(row_ref[...], col_ref[cols, :], NT, preferred_element_type=jnp.float32)
        own_ref[:, cols] += terms[:half]
        acc_ref[:, cols] += terms[half:]

    even, odd = operands[:2], operands[2:]

    @pl.when(step == 0)
    def _():
        @pl.loop(0, parts)
        def _(part):
            build(part, *even)

    for parity, ready, coming in ((1, even, odd), (0, odd, even)):

        @pl.when((step > 0) & (step % 2 == parity))
        def _():
            @pl.loop(0, parts)
            def _(part):
                multiply(part, *ready)
                build(part, *coming)

    @pl.when(step == pl.num_programs(0) - 1)
    def _():
        peer_ref[...] = acc_ref[...].astype(jnp.bfloat16)


def tree(values):
    while len(values) > 1:
        values = [values[i] + values[i + 1] for i in range(0, len(values), 2)]
    return values[0]


def core_sum(value):
    return value + lax.ppermute(value, "core", [(0, 1), (1, 0)])


def all_sum(value, n_z, n_row, n_col, between=None):
    value = core_sum(value)
    far = n_z // 2
    pairs = [[(2 * z + c, 2 * (z ^ (j + c * far)) + c) for z in range(n_z) for c in range(2)] for j in range(far)]
    value = tree([lax.ppermute(value, ("z", "core"), p) for p in pairs])
    if between is not None:
        value = between(value)
    for axis, size in (("row", n_row), ("col", n_col)):
        swaps = [lax.ppermute(value, axis, [(i, i ^ b) for i in range(size)]) for b in range(1, size)]
        value = tree([value] + swaps)
    return core_sum(value)


def per_device(weights, visibility, inverses, grad_points, camera_blocks, grad_cams):
    n_row = lax.axis_size("row")
    n_col = lax.axis_size("col")
    n_z = lax.axis_size("z")
    blocks = 2 * n_z
    z_idx = lax.axis_index("z")
    core_idx = lax.axis_index("core")
    pts_idx = 2 * z_idx + core_idx
    row_idx = lax.axis_index("row")
    col_idx = lax.axis_index("col")
    slots, points = visibility.shape
    width = weights.shape[2]
    strip = width // n_row
    total_rows = blocks * width
    col_count = total_rows // n_col
    set_rows = blocks * strip
    shards = n_row * n_col
    send_rows = 3 * slots * width + AUX
    place = jnp.stack([z_idx, core_idx, row_idx, col_idx]).astype(jnp.int32)
    w_flat = weights.reshape(3 * slots * points, width)
    first_col = (col_idx == 0).astype(jnp.float32)
    lanes = jnp.arange(width, dtype=jnp.int32)[None, :]
    own_lanes = (lanes // strip == row_idx) & (jnp.arange(blocks, dtype=jnp.int32)[:, None] == pts_idx)
    cams_placed = jnp.where(own_lanes, jnp.tile(grad_cams, n_row)[None, :] * first_col, 0.0)
    cam_wide = lax.dynamic_update_slice(
        jnp.zeros((width, width), jnp.float32), camera_blocks * first_col, (row_idx * strip, 0)
    )
    vmem = pl.BlockSpec(memory_space=pltpu.VMEM)
    smem = pl.BlockSpec(memory_space=pltpu.SMEM)
    vec = jax.ShapeDtypeStruct((blocks, width), jnp.float32)
    small = pltpu.CompilerParams(vmem_limit_bytes=16 * 1024 * 1024)

    send, zw, part = pl.pallas_call(
        functools.partial(prepare_kernel, slots, blocks),
        out_shape=(
            jax.ShapeDtypeStruct((send_rows, points), jnp.bfloat16),
            jax.ShapeDtypeStruct((width, 3 * slots * points), jnp.bfloat16),
            vec,
        ),
        in_specs=[vmem] * 5,
        out_specs=(vmem,) * 3,
        compiler_params=small,
        name="prepare",
    )(w_flat, visibility, inverses, grad_points, cams_placed)

    got = lax.all_gather(send, ("row", "col"), axis=0, tiled=False)

    def product(known):
        return pl.pallas_call(
            functools.partial(product_kernel, slots, blocks, len(known)),
            out_shape=vec,
            in_specs=[smem] + [vmem] * (4 + len(known)),
            out_specs=vmem,
            compiler_params=small,
            name="product",
        )(place, visibility, w_flat, zw, cam_wide, *known)

    pair = 2
    half = set_rows // 2
    steps = shards // pair
    make_halves = pl.pallas_call(
        functools.partial(tile_kernel, slots, blocks, width, strip, 2),
        out_shape=(
            jax.ShapeDtypeStruct((half, col_count), jnp.float32),
            jax.ShapeDtypeStruct((half, col_count), jnp.bfloat16),
        ),
        grid=(steps + 1,),
        in_specs=[
            smem,
            pl.BlockSpec((pair, send_rows, points), lambda i: (jnp.minimum(i, steps - 1), 0, 0)),
            pl.BlockSpec((strip, width), lambda i: (0, 0)),
        ],
        out_specs=(
            pl.BlockSpec((half, col_count), lambda i: (0, 0)),
            pl.BlockSpec((half, col_count), lambda i: (0, 0)),
        ),
        scratch_shapes=[
            pltpu.VMEM((half, col_count), jnp.float32),
            pltpu.VMEM((set_rows, 3 * pair * points), jnp.bfloat16),
            pltpu.VMEM((col_count, 3 * pair * points), jnp.bfloat16),
            pltpu.VMEM((set_rows, 3 * pair * points), jnp.bfloat16),
            pltpu.VMEM((col_count, 3 * pair * points), jnp.bfloat16),
        ],
        compiler_params=pltpu.CompilerParams(
            dimension_semantics=("arbitrary",), vmem_limit_bytes=52 * 1024 * 1024
        ),
        cost_estimate=pl.CostEstimate(
            flops=2 * set_rows * col_count * 3 * shards * points,
            bytes_accessed=2 * shards * send_rows * points + 4 * set_rows * col_count,
            transcendentals=0,
        ),
        name="tile",
    )

    held = {}

    def make_tile(value):
        here, value = lax.optimization_barrier((got, value))
        own_half, peer_half = make_halves(place, here, camera_blocks)
        taken = lax.ppermute(peer_half, "core", [(0, 1), (1, 0)])
        tile, value = lax.optimization_barrier((own_half + taken.astype(jnp.float32), value))
        held["schur"] = lax.psum_scatter(tile, "z", scatter_dimension=0, tiled=True)
        return value

    known = [all_sum(part, n_z, n_row, n_col)]
    for between in (None,) * (ITERS - 1) + (make_tile,):
        known.append(all_sum(product(known), n_z, n_row, n_col, between))
    own = jax.ShapeDtypeStruct((1, strip), jnp.float32)
    own_rhs, answer = pl.pallas_call(
        functools.partial(answer_kernel, strip),
        out_shape=(own, own),
        in_specs=[smem] + [vmem] * 4,
        out_specs=(vmem, vmem),
        compiler_params=small,
        name="answer",
    )(place, *known)
    return (held["schur"], own_rhs.reshape(strip), answer.reshape(strip))


def solution(mesh):
    n_pts, n_row, n_col = (mesh.shape[axis] for axis in ("pts", "row", "col"))
    cores = Mesh(mesh.devices.reshape(n_pts // 2, 2, n_row, n_col), ("z", "core", "row", "col"))
    pts = ("z", "core")
    return jax.shard_map(
        per_device,
        mesh=cores,
        in_specs=(
            P(None, (*pts, "row", "col"), None),
            P(None, (*pts, "row", "col")),
            P(None, (*pts, "row", "col")),
            P(None, (*pts, "row", "col")),
            P((*pts, "row"), None),
            P((*pts, "row")),
        ),
        out_specs=(P((*pts, "row"), "col"), P((*pts, "row")), P((*pts, "row"))),
        check_vma=False,
    )
```

```python
import functools

import jax
import jax.numpy as jnp
from jax import lax
from jax.experimental import pallas as pl
from jax.experimental.pallas import tpu as pltpu
from jax.sharding import Mesh
from jax.sharding import PartitionSpec as P

ITERS = 3
NT = (((1,), (1,)), ((), ()))
AUX = 16


def total(first, second):
    return jnp.sum(jnp.sum(first * second, axis=1, keepdims=True), axis=0, keepdims=True)


def minres(rhs_vec, products):
    beta_first = jnp.sqrt(total(rhs_vec, rhs_vec))
    r_older = rhs_vec
    r_old = rhs_vec
    lanczos = rhs_vec
    zero = jnp.zeros_like(beta_first)
    beta_old = zero
    beta_now = beta_first
    d_bar = zero
    eps_now = zero
    phi_bar = beta_first
    cos_now = zero - 1.0
    sin_now = zero
    w_now = jnp.zeros_like(rhs_vec)
    w_old = jnp.zeros_like(rhs_vec)
    answer = jnp.zeros_like(rhs_vec)
    for turn in range(ITERS):
        v_now = lanczos / beta_now
        if turn == len(products):
            return v_now
        lanczos = products[turn]
        if turn > 0:
            lanczos = lanczos - beta_now / beta_old * r_older
        alpha_now = total(v_now, lanczos)
        lanczos = lanczos - alpha_now / beta_now * r_old
        beta_old = beta_now
        beta_now = jnp.sqrt(total(lanczos, lanczos))
        r_older = r_old
        r_old = lanczos
        eps_old = eps_now
        delta_now = cos_now * d_bar + sin_now * alpha_now
        g_bar = sin_now * d_bar - cos_now * alpha_now
        eps_now = sin_now * beta_now
        d_bar = -cos_now * beta_now
        gamma_now = jnp.sqrt(g_bar * g_bar + beta_now * beta_now)
        cos_now = g_bar / gamma_now
        sin_now = beta_now / gamma_now
        phi_now = cos_now * phi_bar
        phi_bar = sin_now * phi_bar
        w_older = w_old
        w_old = w_now
        w_now = (v_now - eps_old * w_older - delta_now * w_old) / gamma_now
        answer = answer + phi_now * w_now
    return answer


def apply_inverse(inv, rows):
    return (
        inv[0] * rows[0] + inv[3] * rows[1] + inv[4] * rows[2],
        inv[3] * rows[0] + inv[1] * rows[1] + inv[5] * rows[2],
        inv[4] * rows[0] + inv[5] * rows[1] + inv[2] * rows[2],
    )


def slot_masks(vis, blocks):
    points = vis.shape[1]
    ids = lax.broadcasted_iota(jnp.int32, (blocks, points), 0)
    return [(vis[k : k + 1, :] == ids).astype(jnp.float32) for k in range(vis.shape[0])]


def prepare_kernel(slots, blocks, w_ref, vis_ref, inv_ref, grad_ref, cams_ref, send_ref, zw_ref, part_ref):
    points = vis_ref.shape[1]
    width = w_ref.shape[1]
    inv = inv_ref[...].astype(jnp.float32)
    inv_rows = [inv[e : e + 1, :] for e in range(6)]
    grad = grad_ref[...].astype(jnp.float32)
    vis = vis_ref[...]
    for k in range(slots):
        turned = []
        for a in range(3):
            at = 3 * k + a
            t = jnp.transpose(w_ref[at * points : (at + 1) * points, :].astype(jnp.float32))
            turned.append(t)
            send_ref[at * width : (at + 1) * width, :] = t.astype(jnp.bfloat16)
        for a, z in enumerate(apply_inverse(inv_rows, turned)):
            at = 3 * k + a
            zw_ref[:, at * points : (at + 1) * points] = z.astype(jnp.bfloat16)
    pad = jnp.zeros((AUX - slots - 6, points), jnp.float32)
    aux = jnp.concatenate([vis.astype(jnp.float32), inv, pad], axis=0)
    send_ref[3 * slots * width :, :] = aux.astype(jnp.bfloat16)
    masks = slot_masks(vis, blocks)
    moved = apply_inverse(inv_rows, [grad[a : a + 1, :] for a in range(3)])
    moved = [e.astype(jnp.bfloat16).astype(jnp.float32) for e in moved]
    lhs = jnp.concatenate([masks[k] * moved[a] for k in range(slots) for a in range(3)], axis=1)
    terms = jnp.dot(lhs.astype(jnp.bfloat16), w_ref[...], preferred_element_type=jnp.float32)
    part_ref[...] = cams_ref[...] - terms


def split(x):
    high = x.astype(jnp.bfloat16)
    low = (x - high.astype(jnp.float32)).astype(jnp.bfloat16)
    return high, low


def product_kernel(slots, blocks, n_known, *refs):
    place_ref, vis_ref, w_ref, zw_ref, cam_ref = refs[:5]
    known = refs[5 : 5 + n_known]
    out_ref = refs[5 + n_known]
    points = vis_ref.shape[1]
    v = minres(known[0][...], [r[...] for r in known[1:]])
    masks = slot_masks(vis_ref[...], blocks)
    v2 = jnp.concatenate(split(v), axis=0)
    dots = jnp.dot(v2, zw_ref[...], preferred_element_type=jnp.float32)
    dots = dots[:blocks] + dots[blocks:]
    t = []
    for a in range(3):
        s = None
        for k in range(slots):
            at = 3 * k + a
            term = masks[k] * dots[:, at * points : (at + 1) * points]
            s = term if s is None else s + term
        t.append(jnp.sum(s, axis=0, keepdims=True))
    lhs = jnp.concatenate([masks[k] * t[a] for k in range(slots) for a in range(3)], axis=1)
    lhs2 = jnp.concatenate(split(lhs), axis=0)
    terms = jnp.dot(lhs2, w_ref[...], preferred_element_type=jnp.float32)
    rows = lax.broadcasted_iota(jnp.int32, v.shape, 0)
    own = jnp.where(rows == 2 * place_ref[0] + place_ref[1], v, 0.0)
    cams = jnp.dot(own, cam_ref[...], precision=lax.Precision.HIGHEST, preferred_element_type=jnp.float32)
    out_ref[...] = cams - terms[:blocks] - terms[blocks:]


def answer_kernel(strip, place_ref, rhs_ref, s1_ref, s2_ref, s3_ref, own_rhs_ref, own_ref):
    rhs = rhs_ref[...]
    answer = minres(rhs, [s1_ref[...], s2_ref[...], s3_ref[...]])
    rows = lax.broadcasted_iota(jnp.int32, rhs.shape, 0)
    for value, ref in ((rhs, own_rhs_ref), (answer, own_ref)):
        line = jnp.sum(jnp.where(rows == 2 * place_ref[0] + place_ref[1], value, 0.0), axis=0, keepdims=True)
        for r in range(rhs.shape[1] // strip):

            @pl.when(place_ref[2] == r)
            def _():
                ref[...] = line[:, r * strip : (r + 1) * strip]


def chosen(picks, terms):
    value = None
    for pick, term in zip(picks, terms):
        part = pick * term
        value = part if value is None else value + part
    return value


def tile_kernel(slots, blocks, width, strip, parts, place_ref, got_ref, cam_ref, own_ref, peer_ref, acc_ref, *operands):
    z_idx, core_idx, row_idx, col_idx = place_ref[0], place_ref[1], place_ref[2], place_ref[3]
    sources, _, points = got_ref.shape
    half, col_count = own_ref.shape
    col_blocks = col_count // width
    base_aux = 3 * slots * width
    fine = 64
    step = pl.program_id(0)

    @pl.when(step == 0)
    def _():
        own_ref[...] = jnp.zeros_like(own_ref)
        acc_ref[...] = jnp.zeros_like(acc_ref)
        for c in range(col_blocks):

            @pl.when(col_idx * col_blocks + c == 2 * z_idx + core_idx)
            def _():
                start = pl.multiple_of(z_idx * strip, strip)
                own_ref[pl.ds(start, strip), c * width : (c + 1) * width] = cam_ref[...]

    def build(part, row_ref, col_ref):
        for s in range(sources):
            aux = got_ref[s, base_aux : base_aux + AUX, :].astype(jnp.float32)
            vis = [aux[k : k + 1, :] for k in range(slots)]
            inv = [aux[slots + e : slots + e + 1, :] for e in range(6)]

            def picks_of(block, one):
                block = block.astype(jnp.float32)
                return [jnp.where(v == block, one, 0.0).astype(jnp.bfloat16) for v in vis]

            col_picks = [picks_of(col_idx * col_blocks + c, 1.0) for c in range(col_blocks)]
            for h in range(0, width // parts, fine):
                terms = []
                for at in range(3 * slots):
                    start = pl.multiple_of(at * width + part * (width // parts) + h, fine)
                    terms.append(got_ref[s, pl.ds(start, fine), :])
                for c in range(col_blocks):
                    rows = [chosen(col_picks[c], terms[a::3]).astype(jnp.float32) for a in range(3)]
                    start = pl.multiple_of(c * width + part * (width // parts) + h, fine)
                    for a, z in enumerate(apply_inverse(inv, rows)):
                        at = (a * sources + s) * points
                        col_ref[pl.ds(start, fine), at : at + points] = z.astype(jnp.bfloat16)
            deep = strip // parts
            terms = []
            for at in range(3 * slots):
                start = pl.multiple_of(at * width + row_idx * strip + part * deep, deep)
                terms.append(got_ref[s, pl.ds(start, deep), :])
            for b in range(blocks):
                other = b >= blocks // 2
                picks = picks_of(2 * (b % (blocks // 2)) + (1 - core_idx if other else core_idx), -1.0)
                start = pl.multiple_of(b * strip + part * deep, deep)
                for a in range(3):
                    at = (a * sources + s) * points
                    row_ref[pl.ds(start, deep), at : at + points] = chosen(picks, terms[a::3])

    def multiply(part, row_ref, col_ref):
        span = col_count // parts
        cols = pl.ds(pl.multiple_of(part * span, span), span)
        terms = lax.dot_general(row_ref[...], col_ref[cols, :], NT, preferred_element_type=jnp.float32)
        own_ref[:, cols] += terms[:half]
        acc_ref[:, cols] += terms[half:]

    even, odd = operands[:2], operands[2:]

    @pl.when(step == 0)
    def _():
        @pl.loop(0, parts)
        def _(part):
            build(part, *even)

    for parity, ready, coming in ((1, even, odd), (0, odd, even)):

        @pl.when((step > 0) & (step % 2 == parity))
        def _():
            @pl.loop(0, parts)
            def _(part):
                multiply(part, *ready)
                build(part, *coming)

    @pl.when(step == pl.num_programs(0) - 1)
    def _():
        peer_ref[...] = acc_ref[...].astype(jnp.bfloat16)


def tree(values):
    while len(values) > 1:
        values = [values[i] + values[i + 1] for i in range(0, len(values), 2)]
    return values[0]


def core_sum(value):
    return value + lax.ppermute(value, "core", [(0, 1), (1, 0)])


def all_sum(value, n_z, n_row, n_col, between=None):
    value = core_sum(value)
    for axis, size, reach in (("row", n_row, n_row), ("col", n_col, n_col), ("z", n_z, min(n_z, 4))):
        far = reach // 2
        by_core, by_place = (1, 2) if axis == "z" else (size, 1)
        pairs = [
            [
                (c * by_core + i * by_place, c * by_core + (i ^ (j + c * far)) * by_place)
                for i in range(size)
                for c in range(2)
            ]
            for j in range(far)
        ]
        axes = ("z", "core") if axis == "z" else ("core", axis)
        value = core_sum(tree([lax.ppermute(value, axes, p) for p in pairs]))
    if between is not None:
        value = between(value)
    bit = 4
    while bit < n_z:
        value = value + lax.ppermute(value, "z", [(i, i ^ bit) for i in range(n_z)])
        bit *= 2
    return value


def per_device(weights, visibility, inverses, grad_points, camera_blocks, grad_cams):
    n_row = lax.axis_size("row")
    n_col = lax.axis_size("col")
    n_z = lax.axis_size("z")
    blocks = 2 * n_z
    z_idx = lax.axis_index("z")
    core_idx = lax.axis_index("core")
    pts_idx = 2 * z_idx + core_idx
    row_idx = lax.axis_index("row")
    col_idx = lax.axis_index("col")
    slots, points = visibility.shape
    width = weights.shape[2]
    strip = width // n_row
    total_rows = blocks * width
    col_count = total_rows // n_col
    set_rows = blocks * strip
    shards = n_row * n_col
    send_rows = 3 * slots * width + AUX
    place = jnp.stack([z_idx, core_idx, row_idx, col_idx]).astype(jnp.int32)
    w_flat = weights.reshape(3 * slots * points, width)
    first_col = (col_idx == 0).astype(jnp.float32)
    lanes = jnp.arange(width, dtype=jnp.int32)[None, :]
    own_lanes = (lanes // strip == row_idx) & (jnp.arange(blocks, dtype=jnp.int32)[:, None] == pts_idx)
    cams_placed = jnp.where(own_lanes, jnp.tile(grad_cams, n_row)[None, :] * first_col, 0.0)
    cam_wide = lax.dynamic_update_slice(
        jnp.zeros((width, width), jnp.float32), camera_blocks * first_col, (row_idx * strip, 0)
    )
    vmem = pl.BlockSpec(memory_space=pltpu.VMEM)
    smem = pl.BlockSpec(memory_space=pltpu.SMEM)
    vec = jax.ShapeDtypeStruct((blocks, width), jnp.float32)
    small = pltpu.CompilerParams(vmem_limit_bytes=16 * 1024 * 1024)

    send, zw, part = pl.pallas_call(
        functools.partial(prepare_kernel, slots, blocks),
        out_shape=(
            jax.ShapeDtypeStruct((send_rows, points), jnp.bfloat16),
            jax.ShapeDtypeStruct((width, 3 * slots * points), jnp.bfloat16),
            vec,
        ),
        in_specs=[vmem] * 5,
        out_specs=(vmem,) * 3,
        name="prepare",
    )(w_flat, visibility, inverses, grad_points, cams_placed)

    got = lax.all_gather(send, ("row", "col"), axis=0, tiled=False)

    def product(known):
        return pl.pallas_call(
            functools.partial(product_kernel, slots, blocks, len(known)),
            out_shape=vec,
            in_specs=[smem] + [vmem] * (4 + len(known)),
            out_specs=vmem,
            compiler_params=small,
            name="product",
        )(place, visibility, w_flat, zw, cam_wide, *known)

    pair = 2
    half = set_rows // 2
    steps = shards // pair
    make_halves = pl.pallas_call(
        functools.partial(tile_kernel, slots, blocks, width, strip, 2),
        out_shape=(
            jax.ShapeDtypeStruct((half, col_count), jnp.float32),
            jax.ShapeDtypeStruct((half, col_count), jnp.bfloat16),
        ),
        grid=(steps + 1,),
        in_specs=[
            smem,
            pl.BlockSpec((pair, send_rows, points), lambda i: (jnp.minimum(i, steps - 1), 0, 0)),
            pl.BlockSpec((strip, width), lambda i: (0, 0)),
        ],
        out_specs=(
            pl.BlockSpec((half, col_count), lambda i: (0, 0)),
            pl.BlockSpec((half, col_count), lambda i: (0, 0)),
        ),
        scratch_shapes=[
            pltpu.VMEM((half, col_count), jnp.float32),
            pltpu.VMEM((set_rows, 3 * pair * points), jnp.bfloat16),
            pltpu.VMEM((col_count, 3 * pair * points), jnp.bfloat16),
            pltpu.VMEM((set_rows, 3 * pair * points), jnp.bfloat16),
            pltpu.VMEM((col_count, 3 * pair * points), jnp.bfloat16),
        ],
        compiler_params=pltpu.CompilerParams(
            dimension_semantics=("arbitrary",), vmem_limit_bytes=52 * 1024 * 1024
        ),
        cost_estimate=pl.CostEstimate(
            flops=2 * set_rows * col_count * 3 * shards * points,
            bytes_accessed=2 * shards * send_rows * points + 4 * set_rows * col_count,
            transcendentals=0,
        ),
        name="tile",
    )

    held = {}

    def make_tile(value):
        here, value = lax.optimization_barrier((got, value))
        own_half, peer_half = make_halves(place, here, camera_blocks)
        taken = lax.ppermute(peer_half, "core", [(0, 1), (1, 0)])
        tile, value = lax.optimization_barrier((own_half + taken.astype(jnp.float32), value))
        held["schur"] = lax.psum_scatter(tile, "z", scatter_dimension=0, tiled=True)
        return value

    known = [all_sum(part, n_z, n_row, n_col)]
    for between in (None,) * (ITERS - 1) + (make_tile,):
        known.append(all_sum(product(known), n_z, n_row, n_col, between))
    own = jax.ShapeDtypeStruct((1, strip), jnp.float32)
    own_rhs, answer = pl.pallas_call(
        functools.partial(answer_kernel, strip),
        out_shape=(own, own),
        in_specs=[smem] + [vmem] * 4,
        out_specs=(vmem, vmem),
        compiler_params=small,
        name="answer",
    )(place, *known)
    return (held["schur"], own_rhs.reshape(strip), answer.reshape(strip))


def solution(mesh):
    n_pts, n_row, n_col = (mesh.shape[axis] for axis in ("pts", "row", "col"))
    cores = Mesh(mesh.devices.reshape(n_pts // 2, 2, n_row, n_col), ("z", "core", "row", "col"))
    pts = ("z", "core")
    return jax.shard_map(
        per_device,
        mesh=cores,
        in_specs=(
            P(None, (*pts, "row", "col"), None),
            P(None, (*pts, "row", "col")),
            P(None, (*pts, "row", "col")),
            P(None, (*pts, "row", "col")),
            P((*pts, "row"), None),
            P((*pts, "row")),
        ),
        out_specs=(P((*pts, "row"), "col"), P((*pts, "row")), P((*pts, "row"))),
        check_vma=False,
    )
```

```python
import functools

import jax
import jax.numpy as jnp
from jax import lax
from jax.experimental import pallas as pl
from jax.experimental.pallas import tpu as pltpu
from jax.sharding import Mesh
from jax.sharding import PartitionSpec as P

ITERS = 3
NT = (((1,), (1,)), ((), ()))
AUX = 16


def total(first, second):
    return jnp.sum(jnp.sum(first * second, axis=1, keepdims=True), axis=0, keepdims=True)


def minres(rhs_vec, products):
    beta_first = jnp.sqrt(total(rhs_vec, rhs_vec))
    r_older = rhs_vec
    r_old = rhs_vec
    lanczos = rhs_vec
    zero = jnp.zeros_like(beta_first)
    beta_old = zero
    beta_now = beta_first
    d_bar = zero
    eps_now = zero
    phi_bar = beta_first
    cos_now = zero - 1.0
    sin_now = zero
    w_now = jnp.zeros_like(rhs_vec)
    w_old = jnp.zeros_like(rhs_vec)
    answer = jnp.zeros_like(rhs_vec)
    for turn in range(ITERS):
        v_now = lanczos / beta_now
        if turn == len(products):
            return v_now
        lanczos = products[turn]
        if turn > 0:
            lanczos = lanczos - beta_now / beta_old * r_older
        alpha_now = total(v_now, lanczos)
        lanczos = lanczos - alpha_now / beta_now * r_old
        beta_old = beta_now
        beta_now = jnp.sqrt(total(lanczos, lanczos))
        r_older = r_old
        r_old = lanczos
        eps_old = eps_now
        delta_now = cos_now * d_bar + sin_now * alpha_now
        g_bar = sin_now * d_bar - cos_now * alpha_now
        eps_now = sin_now * beta_now
        d_bar = -cos_now * beta_now
        gamma_now = jnp.sqrt(g_bar * g_bar + beta_now * beta_now)
        cos_now = g_bar / gamma_now
        sin_now = beta_now / gamma_now
        phi_now = cos_now * phi_bar
        phi_bar = sin_now * phi_bar
        w_older = w_old
        w_old = w_now
        w_now = (v_now - eps_old * w_older - delta_now * w_old) / gamma_now
        answer = answer + phi_now * w_now
    return answer


def apply_inverse(inv, rows):
    return (
        inv[0] * rows[0] + inv[3] * rows[1] + inv[4] * rows[2],
        inv[3] * rows[0] + inv[1] * rows[1] + inv[5] * rows[2],
        inv[4] * rows[0] + inv[5] * rows[1] + inv[2] * rows[2],
    )


def slot_masks(vis, blocks):
    points = vis.shape[1]
    ids = lax.broadcasted_iota(jnp.int32, (blocks, points), 0)
    return [(vis[k : k + 1, :] == ids).astype(jnp.float32) for k in range(vis.shape[0])]


def turned_rows(w_ref, at, points):
    return jnp.transpose(w_ref[at * points : (at + 1) * points, :].astype(jnp.float32))


def send_kernel(slots, w_ref, vis_ref, inv_ref, send_ref):
    points = vis_ref.shape[1]
    width = w_ref.shape[1]
    for at in range(3 * slots):
        send_ref[at * width : (at + 1) * width, :] = turned_rows(w_ref, at, points).astype(jnp.bfloat16)
    pad = jnp.zeros((AUX - slots - 6, points), jnp.float32)
    aux = jnp.concatenate([vis_ref[...].astype(jnp.float32), inv_ref[...].astype(jnp.float32), pad], axis=0)
    send_ref[3 * slots * width :, :] = aux.astype(jnp.bfloat16)


def prepare_kernel(slots, blocks, w_ref, vis_ref, inv_ref, grad_ref, cams_ref, zw_ref, part_ref):
    points = vis_ref.shape[1]
    inv = inv_ref[...].astype(jnp.float32)
    inv_rows = [inv[e : e + 1, :] for e in range(6)]
    grad = grad_ref[...].astype(jnp.float32)
    for k in range(slots):
        turned = [turned_rows(w_ref, 3 * k + a, points) for a in range(3)]
        for a, z in enumerate(apply_inverse(inv_rows, turned)):
            at = 3 * k + a
            zw_ref[:, at * points : (at + 1) * points] = z.astype(jnp.bfloat16)
    masks = slot_masks(vis_ref[...], blocks)
    moved = apply_inverse(inv_rows, [grad[a : a + 1, :] for a in range(3)])
    moved = [e.astype(jnp.bfloat16).astype(jnp.float32) for e in moved]
    lhs = jnp.concatenate([masks[k] * moved[a] for k in range(slots) for a in range(3)], axis=1)
    terms = jnp.dot(lhs.astype(jnp.bfloat16), w_ref[...], preferred_element_type=jnp.float32)
    part_ref[...] = cams_ref[...] - terms


def split(x):
    high = x.astype(jnp.bfloat16)
    low = (x - high.astype(jnp.float32)).astype(jnp.bfloat16)
    return high, low


def product_kernel(slots, blocks, n_known, *refs):
    place_ref, vis_ref, w_ref, zw_ref, cam_ref = refs[:5]
    known = refs[5 : 5 + n_known]
    out_ref = refs[5 + n_known]
    points = vis_ref.shape[1]
    v = minres(known[0][...], [r[...] for r in known[1:]])
    masks = slot_masks(vis_ref[...], blocks)
    v2 = jnp.concatenate(split(v), axis=0)
    dots = jnp.dot(v2, zw_ref[...], preferred_element_type=jnp.float32)
    dots = dots[:blocks] + dots[blocks:]
    t = []
    for a in range(3):
        s = None
        for k in range(slots):
            at = 3 * k + a
            term = masks[k] * dots[:, at * points : (at + 1) * points]
            s = term if s is None else s + term
        t.append(jnp.sum(s, axis=0, keepdims=True))
    lhs = jnp.concatenate([masks[k] * t[a] for k in range(slots) for a in range(3)], axis=1)
    lhs2 = jnp.concatenate(split(lhs), axis=0)
    terms = jnp.dot(lhs2, w_ref[...], preferred_element_type=jnp.float32)
    rows = lax.broadcasted_iota(jnp.int32, v.shape, 0)
    own = jnp.where(rows == 2 * place_ref[0] + place_ref[1], v, 0.0)
    cams = jnp.dot(own, cam_ref[...], precision=lax.Precision.HIGHEST, preferred_element_type=jnp.float32)
    out_ref[...] = cams - terms[:blocks] - terms[blocks:]


def answer_kernel(strip, place_ref, rhs_ref, s1_ref, s2_ref, s3_ref, own_rhs_ref, own_ref):
    rhs = rhs_ref[...]
    answer = minres(rhs, [s1_ref[...], s2_ref[...], s3_ref[...]])
    rows = lax.broadcasted_iota(jnp.int32, rhs.shape, 0)
    for value, ref in ((rhs, own_rhs_ref), (answer, own_ref)):
        line = jnp.sum(jnp.where(rows == 2 * place_ref[0] + place_ref[1], value, 0.0), axis=0, keepdims=True)
        for r in range(rhs.shape[1] // strip):

            @pl.when(place_ref[2] == r)
            def _():
                ref[...] = line[:, r * strip : (r + 1) * strip]


def chosen(picks, terms):
    value = None
    for pick, term in zip(picks, terms):
        part = pick * term
        value = part if value is None else value + part
    return value


def tile_kernel(slots, blocks, width, strip, parts, place_ref, got_ref, cam_ref, own_ref, peer_ref, acc_ref, *operands):
    z_idx, core_idx, row_idx, col_idx = place_ref[0], place_ref[1], place_ref[2], place_ref[3]
    sources, _, points = got_ref.shape
    half, col_count = own_ref.shape
    col_blocks = col_count // width
    base_aux = 3 * slots * width
    fine = 64
    step = pl.program_id(0)

    @pl.when(step == 0)
    def _():
        own_ref[...] = jnp.zeros_like(own_ref)
        acc_ref[...] = jnp.zeros_like(acc_ref)
        for c in range(col_blocks):

            @pl.when(col_idx * col_blocks + c == 2 * z_idx + core_idx)
            def _():
                start = pl.multiple_of(z_idx * strip, strip)
                own_ref[pl.ds(start, strip), c * width : (c + 1) * width] = cam_ref[...]

    def build(part, row_ref, col_ref):
        for s in range(sources):
            aux = got_ref[s, base_aux : base_aux + AUX, :].astype(jnp.float32)
            vis = [aux[k : k + 1, :] for k in range(slots)]
            inv = [aux[slots + e : slots + e + 1, :] for e in range(6)]

            def picks_of(block, one):
                block = block.astype(jnp.float32)
                return [jnp.where(v == block, one, 0.0).astype(jnp.bfloat16) for v in vis]

            col_picks = [picks_of(col_idx * col_blocks + c, 1.0) for c in range(col_blocks)]
            for h in range(0, width // parts, fine):
                terms = []
                for at in range(3 * slots):
                    start = pl.multiple_of(at * width + part * (width // parts) + h, fine)
                    terms.append(got_ref[s, pl.ds(start, fine), :])
                for c in range(col_blocks):
                    rows = [chosen(col_picks[c], terms[a::3]).astype(jnp.float32) for a in range(3)]
                    start = pl.multiple_of(c * width + part * (width // parts) + h, fine)
                    for a, z in enumerate(apply_inverse(inv, rows)):
                        at = (a * sources + s) * points
                        col_ref[pl.ds(start, fine), at : at + points] = z.astype(jnp.bfloat16)
            deep = strip // parts
            terms = []
            for at in range(3 * slots):
                start = pl.multiple_of(at * width + row_idx * strip + part * deep, deep)
                terms.append(got_ref[s, pl.ds(start, deep), :])
            for b in range(blocks):
                other = b >= blocks // 2
                picks = picks_of(2 * (b % (blocks // 2)) + (1 - core_idx if other else core_idx), -1.0)
                start = pl.multiple_of(b * strip + part * deep, deep)
                for a in range(3):
                    at = (a * sources + s) * points
                    row_ref[pl.ds(start, deep), at : at + points] = chosen(picks, terms[a::3])

    def multiply(part, row_ref, col_ref):
        span = col_count // parts
        cols = pl.ds(pl.multiple_of(part * span, span), span)
        terms = lax.dot_general(row_ref[...], col_ref[cols, :], NT, preferred_element_type=jnp.float32)
        own_ref[:, cols] += terms[:half]
        acc_ref[:, cols] += terms[half:]

    even, odd = operands[:2], operands[2:]

    @pl.when(step == 0)
    def _():
        @pl.loop(0, parts)
        def _(part):
            build(part, *even)

    for parity, ready, coming in ((1, even, odd), (0, odd, even)):

        @pl.when((step > 0) & (step % 2 == parity))
        def _():
            @pl.loop(0, parts)
            def _(part):
                multiply(part, *ready)
                build(part, *coming)

    @pl.when(step == pl.num_programs(0) - 1)
    def _():
        peer_ref[...] = acc_ref[...].astype(jnp.bfloat16)


def tree(values):
    while len(values) > 1:
        values = [values[i] + values[i + 1] for i in range(0, len(values), 2)]
    return values[0]


def core_sum(value):
    return value + lax.ppermute(value, "core", [(0, 1), (1, 0)])


def all_sum(value, n_z, n_row, n_col):
    value = core_sum(value)
    far = n_z // 2
    pairs = [[(2 * z + c, 2 * (z ^ (j + c * far)) + c) for z in range(n_z) for c in range(2)] for j in range(far)]
    value = tree([lax.ppermute(value, ("z", "core"), p) for p in pairs])
    for axis, size in (("row", n_row), ("col", n_col)):
        swaps = [lax.ppermute(value, axis, [(i, i ^ b) for i in range(size)]) for b in range(1, size)]
        value = tree([value] + swaps)
    return core_sum(value)


def per_device(weights, visibility, inverses, grad_points, camera_blocks, grad_cams):
    n_row = lax.axis_size("row")
    n_col = lax.axis_size("col")
    n_z = lax.axis_size("z")
    blocks = 2 * n_z
    z_idx = lax.axis_index("z")
    core_idx = lax.axis_index("core")
    pts_idx = 2 * z_idx + core_idx
    row_idx = lax.axis_index("row")
    col_idx = lax.axis_index("col")
    slots, points = visibility.shape
    width = weights.shape[2]
    strip = width // n_row
    total_rows = blocks * width
    col_count = total_rows // n_col
    set_rows = blocks * strip
    shards = n_row * n_col
    send_rows = 3 * slots * width + AUX
    place = jnp.stack([z_idx, core_idx, row_idx, col_idx]).astype(jnp.int32)
    w_flat = weights.reshape(3 * slots * points, width)
    first_col = (col_idx == 0).astype(jnp.float32)
    lanes = jnp.arange(width, dtype=jnp.int32)[None, :]
    own_lanes = (lanes // strip == row_idx) & (jnp.arange(blocks, dtype=jnp.int32)[:, None] == pts_idx)
    cams_placed = jnp.where(own_lanes, jnp.tile(grad_cams, n_row)[None, :] * first_col, 0.0)
    cam_wide = lax.dynamic_update_slice(
        jnp.zeros((width, width), jnp.float32), camera_blocks * first_col, (row_idx * strip, 0)
    )
    vmem = pl.BlockSpec(memory_space=pltpu.VMEM)
    smem = pl.BlockSpec(memory_space=pltpu.SMEM)
    vec = jax.ShapeDtypeStruct((blocks, width), jnp.float32)
    small = pltpu.CompilerParams(vmem_limit_bytes=16 * 1024 * 1024)

    send = pl.pallas_call(
        functools.partial(send_kernel, slots),
        out_shape=jax.ShapeDtypeStruct((send_rows, points), jnp.bfloat16),
        in_specs=[vmem] * 3,
        out_specs=vmem,
        name="send",
    )(w_flat, visibility, inverses)
    got = lax.all_gather(send, ("row", "col"), axis=0, tiled=False)
    zw, part = pl.pallas_call(
        functools.partial(prepare_kernel, slots, blocks),
        out_shape=(jax.ShapeDtypeStruct((width, 3 * slots * points), jnp.bfloat16), vec),
        in_specs=[vmem] * 5,
        out_specs=(vmem, vmem),
        compiler_params=small,
        name="prepare",
    )(w_flat, visibility, inverses, grad_points, cams_placed)

    def product(known):
        return pl.pallas_call(
            functools.partial(product_kernel, slots, blocks, len(known)),
            out_shape=vec,
            in_specs=[smem] + [vmem] * (4 + len(known)),
            out_specs=vmem,
            compiler_params=small,
            name="product",
        )(place, visibility, w_flat, zw, cam_wide, *known)

    pair = 2
    half = set_rows // 2
    steps = shards // pair
    make_halves = pl.pallas_call(
        functools.partial(tile_kernel, slots, blocks, width, strip, 2),
        out_shape=(
            jax.ShapeDtypeStruct((half, col_count), jnp.float32),
            jax.ShapeDtypeStruct((half, col_count), jnp.bfloat16),
        ),
        grid=(steps + 1,),
        in_specs=[
            smem,
            pl.BlockSpec((pair, send_rows, points), lambda i: (jnp.minimum(i, steps - 1), 0, 0)),
            pl.BlockSpec((strip, width), lambda i: (0, 0)),
        ],
        out_specs=(
            pl.BlockSpec((half, col_count), lambda i: (0, 0)),
            pl.BlockSpec((half, col_count), lambda i: (0, 0)),
        ),
        scratch_shapes=[
            pltpu.VMEM((half, col_count), jnp.float32),
            pltpu.VMEM((set_rows, 3 * pair * points), jnp.bfloat16),
            pltpu.VMEM((col_count, 3 * pair * points), jnp.bfloat16),
            pltpu.VMEM((set_rows, 3 * pair * points), jnp.bfloat16),
            pltpu.VMEM((col_count, 3 * pair * points), jnp.bfloat16),
        ],
        compiler_params=pltpu.CompilerParams(
            dimension_semantics=("arbitrary",), vmem_limit_bytes=52 * 1024 * 1024
        ),
        cost_estimate=pl.CostEstimate(
            flops=2 * set_rows * col_count * 3 * shards * points,
            bytes_accessed=2 * shards * send_rows * points + 4 * set_rows * col_count,
            transcendentals=0,
        ),
        name="tile",
    )

    known = [all_sum(part, n_z, n_row, n_col)]
    for _ in range(1, ITERS):
        known.append(all_sum(product(known), n_z, n_row, n_col))
    got, known = lax.optimization_barrier((got, known))
    own_half, peer_half = make_halves(place, got, camera_blocks)
    taken = lax.ppermute(peer_half, "core", [(0, 1), (1, 0)])
    tile, known = lax.optimization_barrier((own_half + taken.astype(jnp.float32), known))
    schur = lax.psum_scatter(tile, "z", scatter_dimension=0, tiled=True)
    known.append(all_sum(product(known), n_z, n_row, n_col))
    own = jax.ShapeDtypeStruct((1, strip), jnp.float32)
    own_rhs, answer = pl.pallas_call(
        functools.partial(answer_kernel, strip),
        out_shape=(own, own),
        in_specs=[smem] + [vmem] * 4,
        out_specs=(vmem, vmem),
        compiler_params=small,
        name="answer",
    )(place, *known)
    return (schur, own_rhs.reshape(strip), answer.reshape(strip))


def solution(mesh):
    n_pts, n_row, n_col = (mesh.shape[axis] for axis in ("pts", "row", "col"))
    cores = Mesh(mesh.devices.reshape(n_pts // 2, 2, n_row, n_col), ("z", "core", "row", "col"))
    pts = ("z", "core")
    return jax.shard_map(
        per_device,
        mesh=cores,
        in_specs=(
            P(None, (*pts, "row", "col"), None),
            P(None, (*pts, "row", "col")),
            P(None, (*pts, "row", "col")),
            P(None, (*pts, "row", "col")),
            P((*pts, "row"), None),
            P((*pts, "row")),
        ),
        out_specs=(P((*pts, "row"), "col"), P((*pts, "row")), P((*pts, "row"))),
        check_vma=False,
    )
```

```python
import functools

import jax
import jax.numpy as jnp
from jax import lax
from jax.experimental import pallas as pl
from jax.experimental.pallas import tpu as pltpu
from jax.sharding import Mesh
from jax.sharding import PartitionSpec as P

ITERS = 3
NT = (((1,), (1,)), ((), ()))
AUX = 16


def total(first, second):
    return jnp.sum(jnp.sum(first * second, axis=1, keepdims=True), axis=0, keepdims=True)


def minres(rhs_vec, products):
    beta_first = jnp.sqrt(total(rhs_vec, rhs_vec))
    r_older = rhs_vec
    r_old = rhs_vec
    lanczos = rhs_vec
    zero = jnp.zeros_like(beta_first)
    beta_old = zero
    beta_now = beta_first
    d_bar = zero
    eps_now = zero
    phi_bar = beta_first
    cos_now = zero - 1.0
    sin_now = zero
    w_now = jnp.zeros_like(rhs_vec)
    w_old = jnp.zeros_like(rhs_vec)
    answer = jnp.zeros_like(rhs_vec)
    for turn in range(ITERS):
        v_now = lanczos / beta_now
        if turn == len(products):
            return v_now
        lanczos = products[turn]
        if turn > 0:
            lanczos = lanczos - beta_now / beta_old * r_older
        alpha_now = total(v_now, lanczos)
        lanczos = lanczos - alpha_now / beta_now * r_old
        beta_old = beta_now
        beta_now = jnp.sqrt(total(lanczos, lanczos))
        r_older = r_old
        r_old = lanczos
        eps_old = eps_now
        delta_now = cos_now * d_bar + sin_now * alpha_now
        g_bar = sin_now * d_bar - cos_now * alpha_now
        eps_now = sin_now * beta_now
        d_bar = -cos_now * beta_now
        gamma_now = jnp.sqrt(g_bar * g_bar + beta_now * beta_now)
        cos_now = g_bar / gamma_now
        sin_now = beta_now / gamma_now
        phi_now = cos_now * phi_bar
        phi_bar = sin_now * phi_bar
        w_older = w_old
        w_old = w_now
        w_now = (v_now - eps_old * w_older - delta_now * w_old) / gamma_now
        answer = answer + phi_now * w_now
    return answer


def apply_inverse(inv, rows):
    return (
        inv[0] * rows[0] + inv[3] * rows[1] + inv[4] * rows[2],
        inv[3] * rows[0] + inv[1] * rows[1] + inv[5] * rows[2],
        inv[4] * rows[0] + inv[5] * rows[1] + inv[2] * rows[2],
    )


def slot_masks(vis, blocks):
    points = vis.shape[1]
    ids = lax.broadcasted_iota(jnp.int32, (blocks, points), 0)
    return [(vis[k : k + 1, :] == ids).astype(jnp.float32) for k in range(vis.shape[0])]


def turned_rows(w_ref, at, points):
    return jnp.transpose(w_ref[at * points : (at + 1) * points, :].astype(jnp.float32))


def send_kernel(slots, w_ref, vis_ref, inv_ref, send_ref):
    points = vis_ref.shape[1]
    width = w_ref.shape[1]
    for at in range(3 * slots):
        send_ref[at * width : (at + 1) * width, :] = turned_rows(w_ref, at, points).astype(jnp.bfloat16)
    pad = jnp.zeros((AUX - slots - 6, points), jnp.float32)
    aux = jnp.concatenate([vis_ref[...].astype(jnp.float32), inv_ref[...].astype(jnp.float32), pad], axis=0)
    send_ref[3 * slots * width :, :] = aux.astype(jnp.bfloat16)


def prepare_kernel(slots, blocks, w_ref, vis_ref, inv_ref, grad_ref, cams_ref, zw_ref, part_ref):
    points = vis_ref.shape[1]
    inv = inv_ref[...].astype(jnp.float32)
    inv_rows = [inv[e : e + 1, :] for e in range(6)]
    grad = grad_ref[...].astype(jnp.float32)
    for k in range(slots):
        turned = [turned_rows(w_ref, 3 * k + a, points) for a in range(3)]
        for a, z in enumerate(apply_inverse(inv_rows, turned)):
            at = 3 * k + a
            zw_ref[:, at * points : (at + 1) * points] = z.astype(jnp.bfloat16)
    masks = slot_masks(vis_ref[...], blocks)
    moved = apply_inverse(inv_rows, [grad[a : a + 1, :] for a in range(3)])
    moved = [e.astype(jnp.bfloat16).astype(jnp.float32) for e in moved]
    lhs = jnp.concatenate([masks[k] * moved[a] for k in range(slots) for a in range(3)], axis=1)
    terms = jnp.dot(lhs.astype(jnp.bfloat16), w_ref[...], preferred_element_type=jnp.float32)
    part_ref[...] = cams_ref[...] - terms


def split(x):
    high = x.astype(jnp.bfloat16)
    low = (x - high.astype(jnp.float32)).astype(jnp.bfloat16)
    return high, low


def product_kernel(slots, blocks, n_known, *refs):
    place_ref, vis_ref, w_ref, zw_ref, cam_ref = refs[:5]
    known = refs[5 : 5 + n_known]
    out_ref = refs[5 + n_known]
    points = vis_ref.shape[1]
    v = minres(known[0][...], [r[...] for r in known[1:]])
    masks = slot_masks(vis_ref[...], blocks)
    v2 = jnp.concatenate(split(v), axis=0)
    dots = jnp.dot(v2, zw_ref[...], preferred_element_type=jnp.float32)
    dots = dots[:blocks] + dots[blocks:]
    t = []
    for a in range(3):
        s = None
        for k in range(slots):
            at = 3 * k + a
            term = masks[k] * dots[:, at * points : (at + 1) * points]
            s = term if s is None else s + term
        t.append(jnp.sum(s, axis=0, keepdims=True))
    lhs = jnp.concatenate([masks[k] * t[a] for k in range(slots) for a in range(3)], axis=1)
    lhs2 = jnp.concatenate(split(lhs), axis=0)
    terms = jnp.dot(lhs2, w_ref[...], preferred_element_type=jnp.float32)
    rows = lax.broadcasted_iota(jnp.int32, v.shape, 0)
    own = jnp.where(rows == 2 * place_ref[0] + place_ref[1], v, 0.0)
    cams = jnp.dot(own, cam_ref[...], precision=lax.Precision.HIGHEST, preferred_element_type=jnp.float32)
    out_ref[...] = cams - terms[:blocks] - terms[blocks:]


def answer_kernel(strip, place_ref, rhs_ref, s1_ref, s2_ref, s3_ref, own_rhs_ref, own_ref):
    rhs = rhs_ref[...]
    answer = minres(rhs, [s1_ref[...], s2_ref[...], s3_ref[...]])
    rows = lax.broadcasted_iota(jnp.int32, rhs.shape, 0)
    for value, ref in ((rhs, own_rhs_ref), (answer, own_ref)):
        line = jnp.sum(jnp.where(rows == 2 * place_ref[0] + place_ref[1], value, 0.0), axis=0, keepdims=True)
        for r in range(rhs.shape[1] // strip):

            @pl.when(place_ref[2] == r)
            def _():
                ref[...] = line[:, r * strip : (r + 1) * strip]


def chosen(picks, terms):
    value = None
    for pick, term in zip(picks, terms):
        part = pick * term
        value = part if value is None else value + part
    return value


def tile_kernel(slots, blocks, width, strip, parts, place_ref, got_ref, cam_ref, own_ref, peer_ref, acc_ref, *operands):
    z_idx, core_idx, row_idx, col_idx = place_ref[0], place_ref[1], place_ref[2], place_ref[3]
    sources, _, points = got_ref.shape
    half, col_count = own_ref.shape
    col_blocks = col_count // width
    base_aux = 3 * slots * width
    fine = 64
    step = pl.program_id(0)

    @pl.when(step == 0)
    def _():
        own_ref[...] = jnp.zeros_like(own_ref)
        acc_ref[...] = jnp.zeros_like(acc_ref)
        for c in range(col_blocks):

            @pl.when(col_idx * col_blocks + c == 2 * z_idx + core_idx)
            def _():
                start = pl.multiple_of(z_idx * strip, strip)
                own_ref[pl.ds(start, strip), c * width : (c + 1) * width] = cam_ref[...]

    def build(part, row_ref, col_ref):
        for s in range(sources):
            aux = got_ref[s, base_aux : base_aux + AUX, :].astype(jnp.float32)
            vis = [aux[k : k + 1, :] for k in range(slots)]
            inv = [aux[slots + e : slots + e + 1, :] for e in range(6)]

            def picks_of(block, one):
                block = block.astype(jnp.float32)
                return [jnp.where(v == block, one, 0.0).astype(jnp.bfloat16) for v in vis]

            col_picks = [picks_of(col_idx * col_blocks + c, 1.0) for c in range(col_blocks)]
            for h in range(0, width // parts, fine):
                terms = []
                for at in range(3 * slots):
                    start = pl.multiple_of(at * width + part * (width // parts) + h, fine)
                    terms.append(got_ref[s, pl.ds(start, fine), :])
                for c in range(col_blocks):
                    rows = [chosen(col_picks[c], terms[a::3]).astype(jnp.float32) for a in range(3)]
                    start = pl.multiple_of(c * width + part * (width // parts) + h, fine)
                    for a, z in enumerate(apply_inverse(inv, rows)):
                        at = (a * sources + s) * points
                        col_ref[pl.ds(start, fine), at : at + points] = z.astype(jnp.bfloat16)
            deep = strip // parts
            terms = []
            for at in range(3 * slots):
                start = pl.multiple_of(at * width + row_idx * strip + part * deep, deep)
                terms.append(got_ref[s, pl.ds(start, deep), :])
            for b in range(blocks):
                other = b >= blocks // 2
                picks = picks_of(2 * (b % (blocks // 2)) + (1 - core_idx if other else core_idx), -1.0)
                start = pl.multiple_of(b * strip + part * deep, deep)
                for a in range(3):
                    at = (a * sources + s) * points
                    row_ref[pl.ds(start, deep), at : at + points] = chosen(picks, terms[a::3])

    def multiply(part, row_ref, col_ref):
        span = col_count // parts
        cols = pl.ds(pl.multiple_of(part * span, span), span)
        terms = lax.dot_general(row_ref[...], col_ref[cols, :], NT, preferred_element_type=jnp.float32)
        own_ref[:, cols] += terms[:half]
        acc_ref[:, cols] += terms[half:]

    even, odd = operands[:2], operands[2:]

    @pl.when(step == 0)
    def _():
        @pl.loop(0, parts)
        def _(part):
            build(part, *even)

    for parity, ready, coming in ((1, even, odd), (0, odd, even)):

        @pl.when((step > 0) & (step % 2 == parity))
        def _():
            @pl.loop(0, parts)
            def _(part):
                multiply(part, *ready)
                build(part, *coming)

    @pl.when(step == pl.num_programs(0) - 1)
    def _():
        peer_ref[...] = acc_ref[...].astype(jnp.bfloat16)


def tree(values):
    while len(values) > 1:
        values = [values[i] + values[i + 1] for i in range(0, len(values), 2)]
    return values[0]


def core_sum(value):
    return value + lax.ppermute(value, "core", [(0, 1), (1, 0)])


def all_sum(value, n_z, n_row, n_col):
    value = core_sum(value)
    far = n_z // 2
    pairs = [[(2 * z + c, 2 * (z ^ (j + c * far)) + c) for z in range(n_z) for c in range(2)] for j in range(far)]
    value = tree([lax.ppermute(value, ("z", "core"), p) for p in pairs])
    for axis, size in (("row", n_row), ("col", n_col)):
        swaps = [lax.ppermute(value, axis, [(i, i ^ b) for i in range(size)]) for b in range(1, size)]
        value = tree([value] + swaps)
    return core_sum(value)


def per_device(weights, visibility, inverses, grad_points, camera_blocks, grad_cams):
    n_row = lax.axis_size("row")
    n_col = lax.axis_size("col")
    n_z = lax.axis_size("z")
    blocks = 2 * n_z
    z_idx = lax.axis_index("z")
    core_idx = lax.axis_index("core")
    pts_idx = 2 * z_idx + core_idx
    row_idx = lax.axis_index("row")
    col_idx = lax.axis_index("col")
    slots, points = visibility.shape
    width = weights.shape[2]
    strip = width // n_row
    total_rows = blocks * width
    col_count = total_rows // n_col
    set_rows = blocks * strip
    shards = n_row * n_col
    send_rows = 3 * slots * width + AUX
    place = jnp.stack([z_idx, core_idx, row_idx, col_idx]).astype(jnp.int32)
    w_flat = weights.reshape(3 * slots * points, width)
    first_col = (col_idx == 0).astype(jnp.float32)
    lanes = jnp.arange(width, dtype=jnp.int32)[None, :]
    own_lanes = (lanes // strip == row_idx) & (jnp.arange(blocks, dtype=jnp.int32)[:, None] == pts_idx)
    cams_placed = jnp.where(own_lanes, jnp.tile(grad_cams, n_row)[None, :] * first_col, 0.0)
    cam_wide = lax.dynamic_update_slice(
        jnp.zeros((width, width), jnp.float32), camera_blocks * first_col, (row_idx * strip, 0)
    )
    vmem = pl.BlockSpec(memory_space=pltpu.VMEM)
    smem = pl.BlockSpec(memory_space=pltpu.SMEM)
    vec = jax.ShapeDtypeStruct((blocks, width), jnp.float32)
    small = pltpu.CompilerParams(vmem_limit_bytes=16 * 1024 * 1024)

    send = pl.pallas_call(
        functools.partial(send_kernel, slots),
        out_shape=jax.ShapeDtypeStruct((send_rows, points), jnp.bfloat16),
        in_specs=[vmem] * 3,
        out_specs=vmem,
        name="send",
    )(w_flat, visibility, inverses)
    got = lax.all_gather(send, ("row", "col"), axis=0, tiled=False)
    zw, part = pl.pallas_call(
        functools.partial(prepare_kernel, slots, blocks),
        out_shape=(jax.ShapeDtypeStruct((width, 3 * slots * points), jnp.bfloat16), vec),
        in_specs=[vmem] * 5,
        out_specs=(vmem, vmem),
        compiler_params=small,
        name="prepare",
    )(w_flat, visibility, inverses, grad_points, cams_placed)

    def product(known):
        return pl.pallas_call(
            functools.partial(product_kernel, slots, blocks, len(known)),
            out_shape=vec,
            in_specs=[smem] + [vmem] * (4 + len(known)),
            out_specs=vmem,
            compiler_params=small,
            name="product",
        )(place, visibility, w_flat, zw, cam_wide, *known)

    pair = 2
    half = set_rows // 2
    steps = shards // pair
    make_halves = pl.pallas_call(
        functools.partial(tile_kernel, slots, blocks, width, strip, 2),
        out_shape=(
            jax.ShapeDtypeStruct((half, col_count), jnp.float32),
            jax.ShapeDtypeStruct((half, col_count), jnp.bfloat16),
        ),
        grid=(steps + 1,),
        in_specs=[
            smem,
            pl.BlockSpec((pair, send_rows, points), lambda i: (jnp.minimum(i, steps - 1), 0, 0)),
            pl.BlockSpec((strip, width), lambda i: (0, 0)),
        ],
        out_specs=(
            pl.BlockSpec((half, col_count), lambda i: (0, 0)),
            pl.BlockSpec((half, col_count), lambda i: (0, 0)),
        ),
        scratch_shapes=[
            pltpu.VMEM((half, col_count), jnp.float32),
            pltpu.VMEM((set_rows, 3 * pair * points), jnp.bfloat16),
            pltpu.VMEM((col_count, 3 * pair * points), jnp.bfloat16),
            pltpu.VMEM((set_rows, 3 * pair * points), jnp.bfloat16),
            pltpu.VMEM((col_count, 3 * pair * points), jnp.bfloat16),
        ],
        compiler_params=pltpu.CompilerParams(
            dimension_semantics=("arbitrary",), vmem_limit_bytes=50 * 1024 * 1024
        ),
        cost_estimate=pl.CostEstimate(
            flops=2 * set_rows * col_count * 3 * shards * points,
            bytes_accessed=2 * shards * send_rows * points + 4 * set_rows * col_count,
            transcendentals=0,
        ),
        name="tile",
    )

    known = [all_sum(part, n_z, n_row, n_col)]
    for _ in range(1, ITERS):
        known.append(all_sum(product(known), n_z, n_row, n_col))
    got, known = lax.optimization_barrier((got, known))
    own_half, peer_half = make_halves(place, got, camera_blocks)
    taken = lax.ppermute(peer_half, "core", [(0, 1), (1, 0)])
    tile, known = lax.optimization_barrier((own_half + taken.astype(jnp.float32), known))
    schur = lax.psum_scatter(tile, "z", scatter_dimension=0, tiled=True)
    known.append(all_sum(product(known), n_z, n_row, n_col))
    own = jax.ShapeDtypeStruct((1, strip), jnp.float32)
    own_rhs, answer = pl.pallas_call(
        functools.partial(answer_kernel, strip),
        out_shape=(own, own),
        in_specs=[smem] + [vmem] * 4,
        out_specs=(vmem, vmem),
        compiler_params=small,
        name="answer",
    )(place, *known)
    return (schur, own_rhs.reshape(strip), answer.reshape(strip))


def solution(mesh):
    n_pts, n_row, n_col = (mesh.shape[axis] for axis in ("pts", "row", "col"))
    cores = Mesh(mesh.devices.reshape(n_pts // 2, 2, n_row, n_col), ("z", "core", "row", "col"))
    pts = ("z", "core")
    return jax.shard_map(
        per_device,
        mesh=cores,
        in_specs=(
            P(None, (*pts, "row", "col"), None),
            P(None, (*pts, "row", "col")),
            P(None, (*pts, "row", "col")),
            P(None, (*pts, "row", "col")),
            P((*pts, "row"), None),
            P((*pts, "row")),
        ),
        out_specs=(P((*pts, "row"), "col"), P((*pts, "row")), P((*pts, "row"))),
        check_vma=False,
    )
```

```python
import functools

import jax
import jax.numpy as jnp
from jax import lax
from jax.experimental import pallas as pl
from jax.experimental.pallas import tpu as pltpu
from jax.sharding import Mesh
from jax.sharding import PartitionSpec as P

ITERS = 3
NT = (((1,), (1,)), ((), ()))
AUX = 16


def total(first, second):
    return jnp.sum(jnp.sum(first * second, axis=1, keepdims=True), axis=0, keepdims=True)


def minres(rhs_vec, products):
    beta_first = jnp.sqrt(total(rhs_vec, rhs_vec))
    r_older = rhs_vec
    r_old = rhs_vec
    lanczos = rhs_vec
    zero = jnp.zeros_like(beta_first)
    beta_old = zero
    beta_now = beta_first
    d_bar = zero
    eps_now = zero
    phi_bar = beta_first
    cos_now = zero - 1.0
    sin_now = zero
    w_now = jnp.zeros_like(rhs_vec)
    w_old = jnp.zeros_like(rhs_vec)
    answer = jnp.zeros_like(rhs_vec)
    for turn in range(ITERS):
        v_now = lanczos / beta_now
        if turn == len(products):
            return v_now
        lanczos = products[turn]
        if turn > 0:
            lanczos = lanczos - beta_now / beta_old * r_older
        alpha_now = total(v_now, lanczos)
        lanczos = lanczos - alpha_now / beta_now * r_old
        beta_old = beta_now
        beta_now = jnp.sqrt(total(lanczos, lanczos))
        r_older = r_old
        r_old = lanczos
        eps_old = eps_now
        delta_now = cos_now * d_bar + sin_now * alpha_now
        g_bar = sin_now * d_bar - cos_now * alpha_now
        eps_now = sin_now * beta_now
        d_bar = -cos_now * beta_now
        gamma_now = jnp.sqrt(g_bar * g_bar + beta_now * beta_now)
        cos_now = g_bar / gamma_now
        sin_now = beta_now / gamma_now
        phi_now = cos_now * phi_bar
        phi_bar = sin_now * phi_bar
        w_older = w_old
        w_old = w_now
        w_now = (v_now - eps_old * w_older - delta_now * w_old) / gamma_now
        answer = answer + phi_now * w_now
    return answer


def apply_inverse(inv, rows):
    return (
        inv[0] * rows[0] + inv[3] * rows[1] + inv[4] * rows[2],
        inv[3] * rows[0] + inv[1] * rows[1] + inv[5] * rows[2],
        inv[4] * rows[0] + inv[5] * rows[1] + inv[2] * rows[2],
    )


def slot_masks(vis, blocks):
    points = vis.shape[1]
    ids = lax.broadcasted_iota(jnp.int32, (blocks, points), 0)
    return [(vis[k : k + 1, :] == ids).astype(jnp.float32) for k in range(vis.shape[0])]


def turned_rows(w_ref, at, points):
    return jnp.transpose(w_ref[at * points : (at + 1) * points, :].astype(jnp.float32))


def send_kernel(slots, w_ref, vis_ref, inv_ref, send_ref):
    points = vis_ref.shape[1]
    width = w_ref.shape[1]
    for at in range(3 * slots):
        send_ref[at * width : (at + 1) * width, :] = turned_rows(w_ref, at, points).astype(jnp.bfloat16)
    pad = jnp.zeros((AUX - slots - 6, points), jnp.float32)
    aux = jnp.concatenate([vis_ref[...].astype(jnp.float32), inv_ref[...].astype(jnp.float32), pad], axis=0)
    send_ref[3 * slots * width :, :] = aux.astype(jnp.bfloat16)


def prepare_kernel(slots, blocks, w_ref, vis_ref, inv_ref, grad_ref, cams_ref, zw_ref, part_ref):
    points = vis_ref.shape[1]
    inv = inv_ref[...].astype(jnp.float32)
    inv_rows = [inv[e : e + 1, :] for e in range(6)]
    grad = grad_ref[...].astype(jnp.float32)
    for k in range(slots):
        turned = [turned_rows(w_ref, 3 * k + a, points) for a in range(3)]
        for a, z in enumerate(apply_inverse(inv_rows, turned)):
            at = 3 * k + a
            zw_ref[:, at * points : (at + 1) * points] = z.astype(jnp.bfloat16)
    masks = slot_masks(vis_ref[...], blocks)
    moved = apply_inverse(inv_rows, [grad[a : a + 1, :] for a in range(3)])
    moved = [e.astype(jnp.bfloat16).astype(jnp.float32) for e in moved]
    lhs = jnp.concatenate([masks[k] * moved[a] for k in range(slots) for a in range(3)], axis=1)
    terms = jnp.dot(lhs.astype(jnp.bfloat16), w_ref[...], preferred_element_type=jnp.float32)
    part_ref[...] = cams_ref[...] - terms


def split(x):
    high = x.astype(jnp.bfloat16)
    low = (x - high.astype(jnp.float32)).astype(jnp.bfloat16)
    return high, low


def product_kernel(slots, blocks, n_known, *refs):
    place_ref, vis_ref, w_ref, zw_ref, cam_ref = refs[:5]
    known = refs[5 : 5 + n_known]
    out_ref = refs[5 + n_known]
    points = vis_ref.shape[1]
    v = minres(known[0][...], [r[...] for r in known[1:]])
    masks = slot_masks(vis_ref[...], blocks)
    v2 = jnp.concatenate(split(v), axis=0)
    dots = jnp.dot(v2, zw_ref[...], preferred_element_type=jnp.float32)
    dots = dots[:blocks] + dots[blocks:]
    t = []
    for a in range(3):
        s = None
        for k in range(slots):
            at = 3 * k + a
            term = masks[k] * dots[:, at * points : (at + 1) * points]
            s = term if s is None else s + term
        t.append(jnp.sum(s, axis=0, keepdims=True))
    lhs = jnp.concatenate([masks[k] * t[a] for k in range(slots) for a in range(3)], axis=1)
    lhs2 = jnp.concatenate(split(lhs), axis=0)
    terms = jnp.dot(lhs2, w_ref[...], preferred_element_type=jnp.float32)
    rows = lax.broadcasted_iota(jnp.int32, v.shape, 0)
    own = jnp.where(rows == 2 * place_ref[0] + place_ref[1], v, 0.0)
    cams = jnp.dot(own, cam_ref[...], precision=lax.Precision.HIGHEST, preferred_element_type=jnp.float32)
    out_ref[...] = cams - terms[:blocks] - terms[blocks:]


def answer_kernel(strip, place_ref, rhs_ref, s1_ref, s2_ref, s3_ref, own_rhs_ref, own_ref):
    rhs = rhs_ref[...]
    answer = minres(rhs, [s1_ref[...], s2_ref[...], s3_ref[...]])
    rows = lax.broadcasted_iota(jnp.int32, rhs.shape, 0)
    for value, ref in ((rhs, own_rhs_ref), (answer, own_ref)):
        line = jnp.sum(jnp.where(rows == 2 * place_ref[0] + place_ref[1], value, 0.0), axis=0, keepdims=True)
        for r in range(rhs.shape[1] // strip):

            @pl.when(place_ref[2] == r)
            def _():
                ref[...] = line[:, r * strip : (r + 1) * strip]


def chosen(picks, terms):
    value = None
    for pick, term in zip(picks, terms):
        part = pick * term
        value = part if value is None else value + part
    return value


def tile_kernel(slots, blocks, width, strip, parts, place_ref, got_ref, own_ref, peer_ref, acc_ref, *operands):
    core_idx, row_idx, col_idx = place_ref[1], place_ref[2], place_ref[3]
    sources, _, points = got_ref.shape
    half, col_count = own_ref.shape
    col_blocks = col_count // width
    base_aux = 3 * slots * width
    fine = 64
    step = pl.program_id(0)

    @pl.when(step == 0)
    def _():
        own_ref[...] = jnp.zeros_like(own_ref)
        acc_ref[...] = jnp.zeros_like(acc_ref)

    def build(part, row_ref, col_ref):
        for s in range(sources):
            aux = got_ref[s, base_aux : base_aux + AUX, :].astype(jnp.float32)
            vis = [aux[k : k + 1, :] for k in range(slots)]
            inv = [aux[slots + e : slots + e + 1, :] for e in range(6)]

            def picks_of(block, one):
                block = block.astype(jnp.float32)
                return [jnp.where(v == block, one, 0.0).astype(jnp.bfloat16) for v in vis]

            col_picks = [picks_of(col_idx * col_blocks + c, 1.0) for c in range(col_blocks)]
            for h in range(0, width // parts, fine):
                terms = []
                for at in range(3 * slots):
                    start = pl.multiple_of(at * width + part * (width // parts) + h, fine)
                    terms.append(got_ref[s, pl.ds(start, fine), :])
                for c in range(col_blocks):
                    rows = [chosen(col_picks[c], terms[a::3]).astype(jnp.float32) for a in range(3)]
                    start = pl.multiple_of(c * width + part * (width // parts) + h, fine)
                    for a, z in enumerate(apply_inverse(inv, rows)):
                        at = (a * sources + s) * points
                        col_ref[pl.ds(start, fine), at : at + points] = z.astype(jnp.bfloat16)
            deep = strip // parts
            terms = []
            for at in range(3 * slots):
                start = pl.multiple_of(at * width + row_idx * strip + part * deep, deep)
                terms.append(got_ref[s, pl.ds(start, deep), :])
            for b in range(blocks):
                other = b >= blocks // 2
                picks = picks_of(2 * (b % (blocks // 2)) + (1 - core_idx if other else core_idx), -1.0)
                start = pl.multiple_of(b * strip + part * deep, deep)
                for a in range(3):
                    at = (a * sources + s) * points
                    row_ref[pl.ds(start, deep), at : at + points] = chosen(picks, terms[a::3])

    def multiply(part, row_ref, col_ref):
        span = col_count // parts
        cols = pl.ds(pl.multiple_of(part * span, span), span)
        terms = lax.dot_general(row_ref[...], col_ref[cols, :], NT, preferred_element_type=jnp.float32)
        own_ref[:, cols] += terms[:half]
        acc_ref[:, cols] += terms[half:]

    even, odd = operands[:2], operands[2:]

    @pl.when(step == 0)
    def _():
        @pl.loop(0, parts)
        def _(part):
            build(part, *even)

    for parity, ready, coming in ((1, even, odd), (0, odd, even)):

        @pl.when((step > 0) & (step % 2 == parity))
        def _():
            @pl.loop(0, parts)
            def _(part):
                multiply(part, *ready)
                build(part, *coming)

    @pl.when(step == pl.num_programs(0) - 1)
    def _():
        peer_ref[...] = acc_ref[...].astype(jnp.bfloat16)


def tree(values):
    while len(values) > 1:
        values = [values[i] + values[i + 1] for i in range(0, len(values), 2)]
    return values[0]


def core_sum(value):
    return value + lax.ppermute(value, "core", [(0, 1), (1, 0)])


def all_sum(value, n_z, n_row, n_col):
    value = core_sum(value)
    far = n_z // 2
    pairs = [[(2 * z + c, 2 * (z ^ (j + c * far)) + c) for z in range(n_z) for c in range(2)] for j in range(far)]
    value = tree([lax.ppermute(value, ("z", "core"), p) for p in pairs])
    for axis, size in (("row", n_row), ("col", n_col)):
        swaps = [lax.ppermute(value, axis, [(i, i ^ b) for i in range(size)]) for b in range(1, size)]
        value = tree([value] + swaps)
    return core_sum(value)


def per_device(weights, visibility, inverses, grad_points, camera_blocks, grad_cams):
    n_row = lax.axis_size("row")
    n_col = lax.axis_size("col")
    n_z = lax.axis_size("z")
    blocks = 2 * n_z
    z_idx = lax.axis_index("z")
    core_idx = lax.axis_index("core")
    pts_idx = 2 * z_idx + core_idx
    row_idx = lax.axis_index("row")
    col_idx = lax.axis_index("col")
    slots, points = visibility.shape
    width = weights.shape[2]
    strip = width // n_row
    total_rows = blocks * width
    col_count = total_rows // n_col
    set_rows = blocks * strip
    shards = n_row * n_col
    send_rows = 3 * slots * width + AUX
    place = jnp.stack([z_idx, core_idx, row_idx, col_idx]).astype(jnp.int32)
    w_flat = weights.reshape(3 * slots * points, width)
    first_col = (col_idx == 0).astype(jnp.float32)
    lanes = jnp.arange(width, dtype=jnp.int32)[None, :]
    own_lanes = (lanes // strip == row_idx) & (jnp.arange(blocks, dtype=jnp.int32)[:, None] == pts_idx)
    cams_placed = jnp.where(own_lanes, jnp.tile(grad_cams, n_row)[None, :] * first_col, 0.0)
    cam_wide = lax.dynamic_update_slice(
        jnp.zeros((width, width), jnp.float32), camera_blocks * first_col, (row_idx * strip, 0)
    )
    vmem = pl.BlockSpec(memory_space=pltpu.VMEM)
    smem = pl.BlockSpec(memory_space=pltpu.SMEM)
    vec = jax.ShapeDtypeStruct((blocks, width), jnp.float32)
    small = pltpu.CompilerParams(vmem_limit_bytes=16 * 1024 * 1024)

    send = pl.pallas_call(
        functools.partial(send_kernel, slots),
        out_shape=jax.ShapeDtypeStruct((send_rows, points), jnp.bfloat16),
        in_specs=[vmem] * 3,
        out_specs=vmem,
        name="send",
    )(w_flat, visibility, inverses)
    got = lax.all_gather(send, ("row", "col"), axis=0, tiled=False)
    zw, part = pl.pallas_call(
        functools.partial(prepare_kernel, slots, blocks),
        out_shape=(jax.ShapeDtypeStruct((width, 3 * slots * points), jnp.bfloat16), vec),
        in_specs=[vmem] * 5,
        out_specs=(vmem, vmem),
        compiler_params=small,
        name="prepare",
    )(w_flat, visibility, inverses, grad_points, cams_placed)

    def product(known):
        return pl.pallas_call(
            functools.partial(product_kernel, slots, blocks, len(known)),
            out_shape=vec,
            in_specs=[smem] + [vmem] * (4 + len(known)),
            out_specs=vmem,
            compiler_params=small,
            name="product",
        )(place, visibility, w_flat, zw, cam_wide, *known)

    pair = 2
    half = set_rows // 2
    steps = shards // pair
    make_halves = pl.pallas_call(
        functools.partial(tile_kernel, slots, blocks, width, strip, 2),
        out_shape=(
            jax.ShapeDtypeStruct((half, col_count), jnp.float32),
            jax.ShapeDtypeStruct((half, col_count), jnp.bfloat16),
        ),
        grid=(steps + 1,),
        in_specs=[
            smem,
            pl.BlockSpec((pair, send_rows, points), lambda i: (jnp.minimum(i, steps - 1), 0, 0)),
        ],
        out_specs=(
            pl.BlockSpec((half, col_count), lambda i: (0, 0)),
            pl.BlockSpec((half, col_count), lambda i: (0, 0)),
        ),
        scratch_shapes=[
            pltpu.VMEM((half, col_count), jnp.float32),
            pltpu.VMEM((set_rows, 3 * pair * points), jnp.bfloat16),
            pltpu.VMEM((col_count, 3 * pair * points), jnp.bfloat16),
            pltpu.VMEM((set_rows, 3 * pair * points), jnp.bfloat16),
            pltpu.VMEM((col_count, 3 * pair * points), jnp.bfloat16),
        ],
        compiler_params=pltpu.CompilerParams(
            dimension_semantics=("arbitrary",), vmem_limit_bytes=50 * 1024 * 1024
        ),
        cost_estimate=pl.CostEstimate(
            flops=2 * set_rows * col_count * 3 * shards * points,
            bytes_accessed=2 * shards * send_rows * points + 4 * set_rows * col_count,
            transcendentals=0,
        ),
        name="tile",
    )

    known = [all_sum(part, n_z, n_row, n_col)]
    for _ in range(1, ITERS):
        known.append(all_sum(product(known), n_z, n_row, n_col))
    got, known = lax.optimization_barrier((got, known))
    own_half, peer_half = make_halves(place, got)
    taken = lax.ppermute(peer_half, "core", [(0, 1), (1, 0)])
    tile, known = lax.optimization_barrier(((own_half + taken.astype(jnp.float32)).astype(jnp.bfloat16), known))
    minus_g = lax.psum_scatter(tile, "z", scatter_dimension=0, tiled=True)
    col_blocks = col_count // width
    block_at = jnp.arange(col_count, dtype=jnp.int32)[None, :] // width + col_idx * col_blocks
    cams = jnp.where(block_at == pts_idx, jnp.tile(camera_blocks, (1, col_blocks)), 0.0)
    schur = minus_g.astype(jnp.float32) + cams
    known.append(all_sum(product(known), n_z, n_row, n_col))
    own = jax.ShapeDtypeStruct((1, strip), jnp.float32)
    own_rhs, answer = pl.pallas_call(
        functools.partial(answer_kernel, strip),
        out_shape=(own, own),
        in_specs=[smem] + [vmem] * 4,
        out_specs=(vmem, vmem),
        compiler_params=small,
        name="answer",
    )(place, *known)
    return (schur, own_rhs.reshape(strip), answer.reshape(strip))


def solution(mesh):
    n_pts, n_row, n_col = (mesh.shape[axis] for axis in ("pts", "row", "col"))
    cores = Mesh(mesh.devices.reshape(n_pts // 2, 2, n_row, n_col), ("z", "core", "row", "col"))
    pts = ("z", "core")
    return jax.shard_map(
        per_device,
        mesh=cores,
        in_specs=(
            P(None, (*pts, "row", "col"), None),
            P(None, (*pts, "row", "col")),
            P(None, (*pts, "row", "col")),
            P(None, (*pts, "row", "col")),
            P((*pts, "row"), None),
            P((*pts, "row")),
        ),
        out_specs=(P((*pts, "row"), "col"), P((*pts, "row")), P((*pts, "row"))),
        check_vma=False,
    )
```

```python
import functools

import jax
import jax.numpy as jnp
from jax import lax
from jax.experimental import pallas as pl
from jax.experimental.pallas import tpu as pltpu
from jax.sharding import Mesh
from jax.sharding import PartitionSpec as P

ITERS = 3
NT = (((1,), (1,)), ((), ()))
AUX = 16


def total(first, second):
    return jnp.sum(jnp.sum(first * second, axis=1, keepdims=True), axis=0, keepdims=True)


def minres(rhs_vec, products):
    beta_first = jnp.sqrt(total(rhs_vec, rhs_vec))
    r_older = rhs_vec
    r_old = rhs_vec
    lanczos = rhs_vec
    zero = jnp.zeros_like(beta_first)
    beta_old = zero
    beta_now = beta_first
    d_bar = zero
    eps_now = zero
    phi_bar = beta_first
    cos_now = zero - 1.0
    sin_now = zero
    w_now = jnp.zeros_like(rhs_vec)
    w_old = jnp.zeros_like(rhs_vec)
    answer = jnp.zeros_like(rhs_vec)
    for turn in range(ITERS):
        v_now = lanczos / beta_now
        if turn == len(products):
            return v_now
        lanczos = products[turn]
        if turn > 0:
            lanczos = lanczos - beta_now / beta_old * r_older
        alpha_now = total(v_now, lanczos)
        lanczos = lanczos - alpha_now / beta_now * r_old
        beta_old = beta_now
        beta_now = jnp.sqrt(total(lanczos, lanczos))
        r_older = r_old
        r_old = lanczos
        eps_old = eps_now
        delta_now = cos_now * d_bar + sin_now * alpha_now
        g_bar = sin_now * d_bar - cos_now * alpha_now
        eps_now = sin_now * beta_now
        d_bar = -cos_now * beta_now
        gamma_now = jnp.sqrt(g_bar * g_bar + beta_now * beta_now)
        cos_now = g_bar / gamma_now
        sin_now = beta_now / gamma_now
        phi_now = cos_now * phi_bar
        phi_bar = sin_now * phi_bar
        w_older = w_old
        w_old = w_now
        w_now = (v_now - eps_old * w_older - delta_now * w_old) / gamma_now
        answer = answer + phi_now * w_now
    return answer


def apply_inverse(inv, rows):
    return (
        inv[0] * rows[0] + inv[3] * rows[1] + inv[4] * rows[2],
        inv[3] * rows[0] + inv[1] * rows[1] + inv[5] * rows[2],
        inv[4] * rows[0] + inv[5] * rows[1] + inv[2] * rows[2],
    )


def slot_masks(vis, blocks):
    points = vis.shape[1]
    ids = lax.broadcasted_iota(jnp.int32, (blocks, points), 0)
    return [(vis[k : k + 1, :] == ids).astype(jnp.float32) for k in range(vis.shape[0])]


def turned_rows(w_ref, at, points):
    return jnp.transpose(w_ref[at * points : (at + 1) * points, :].astype(jnp.float32))


def send_kernel(slots, w_ref, vis_ref, inv_ref, send_ref, held_ref, made_ref, in_sem, out_sem):
    points = vis_ref.shape[1]
    width = w_ref.shape[1]
    rows, made = 3 * points, 3 * width
    arrivals, leaves = [], []
    for k in range(slots):
        span = pl.ds(k * rows, rows)
        arrivals.append(pltpu.make_async_copy(w_ref.at[span, :], held_ref.at[span, :], in_sem.at[k]))
        arrivals[k].start()
    pad = jnp.zeros((AUX - slots - 6, points), jnp.float32)
    aux = jnp.concatenate([vis_ref[...].astype(jnp.float32), inv_ref[...].astype(jnp.float32), pad], axis=0)
    made_ref[slots * made :, :] = aux.astype(jnp.bfloat16)
    for k in range(slots + 1):
        if k < slots:
            arrivals[k].wait()
            for at in range(3 * k, 3 * k + 3):
                made_ref[at * width : (at + 1) * width, :] = turned_rows(held_ref, at, points).astype(jnp.bfloat16)
        span = pl.ds(k * made, made if k < slots else AUX)
        leaves.append(pltpu.make_async_copy(made_ref.at[span, :], send_ref.at[span, :], out_sem.at[k]))
        leaves[k].start()
    for leave in leaves:
        leave.wait()


def prepare_kernel(slots, blocks, w_ref, vis_ref, inv_ref, grad_ref, cams_ref, zw_ref, part_ref):
    points = vis_ref.shape[1]
    inv = inv_ref[...].astype(jnp.float32)
    inv_rows = [inv[e : e + 1, :] for e in range(6)]
    grad = grad_ref[...].astype(jnp.float32)
    for k in range(slots):
        turned = [turned_rows(w_ref, 3 * k + a, points) for a in range(3)]
        for a, z in enumerate(apply_inverse(inv_rows, turned)):
            at = 3 * k + a
            zw_ref[:, at * points : (at + 1) * points] = z.astype(jnp.bfloat16)
    masks = slot_masks(vis_ref[...], blocks)
    moved = apply_inverse(inv_rows, [grad[a : a + 1, :] for a in range(3)])
    moved = [e.astype(jnp.bfloat16).astype(jnp.float32) for e in moved]
    lhs = jnp.concatenate([masks[k] * moved[a] for k in range(slots) for a in range(3)], axis=1)
    terms = jnp.dot(lhs.astype(jnp.bfloat16), w_ref[...], preferred_element_type=jnp.float32)
    part_ref[...] = cams_ref[...] - terms


def split(x):
    high = x.astype(jnp.bfloat16)
    low = (x - high.astype(jnp.float32)).astype(jnp.bfloat16)
    return high, low


def product_kernel(slots, blocks, n_known, *refs):
    place_ref, vis_ref, w_ref, zw_ref, cam_ref = refs[:5]
    known = refs[5 : 5 + n_known]
    out_ref = refs[5 + n_known]
    points = vis_ref.shape[1]
    v = minres(known[0][...], [r[...] for r in known[1:]])
    masks = slot_masks(vis_ref[...], blocks)
    v2 = jnp.concatenate(split(v), axis=0)
    dots = jnp.dot(v2, zw_ref[...], preferred_element_type=jnp.float32)
    dots = dots[:blocks] + dots[blocks:]
    t = []
    for a in range(3):
        s = None
        for k in range(slots):
            at = 3 * k + a
            term = masks[k] * dots[:, at * points : (at + 1) * points]
            s = term if s is None else s + term
        t.append(jnp.sum(s, axis=0, keepdims=True))
    lhs = jnp.concatenate([masks[k] * t[a] for k in range(slots) for a in range(3)], axis=1)
    lhs2 = jnp.concatenate(split(lhs), axis=0)
    terms = jnp.dot(lhs2, w_ref[...], preferred_element_type=jnp.float32)
    rows = lax.broadcasted_iota(jnp.int32, v.shape, 0)
    own = jnp.where(rows == 2 * place_ref[0] + place_ref[1], v, 0.0)
    cams = jnp.dot(own, cam_ref[...], precision=lax.Precision.HIGHEST, preferred_element_type=jnp.float32)
    out_ref[...] = cams - terms[:blocks] - terms[blocks:]


def answer_kernel(strip, place_ref, rhs_ref, s1_ref, s2_ref, s3_ref, own_rhs_ref, own_ref):
    rhs = rhs_ref[...]
    answer = minres(rhs, [s1_ref[...], s2_ref[...], s3_ref[...]])
    rows = lax.broadcasted_iota(jnp.int32, rhs.shape, 0)
    for value, ref in ((rhs, own_rhs_ref), (answer, own_ref)):
        line = jnp.sum(jnp.where(rows == 2 * place_ref[0] + place_ref[1], value, 0.0), axis=0, keepdims=True)
        for r in range(rhs.shape[1] // strip):

            @pl.when(place_ref[2] == r)
            def _():
                ref[...] = line[:, r * strip : (r + 1) * strip]


def chosen(picks, terms):
    value = None
    for pick, term in zip(picks, terms):
        part = pick * term
        value = part if value is None else value + part
    return value


def tile_kernel(slots, blocks, width, strip, parts, place_ref, got_ref, cam_ref, own_ref, peer_ref, acc_ref, *operands):
    z_idx, core_idx, row_idx, col_idx = place_ref[0], place_ref[1], place_ref[2], place_ref[3]
    sources, _, points = got_ref.shape
    half, col_count = own_ref.shape
    col_blocks = col_count // width
    base_aux = 3 * slots * width
    fine = 64
    step = pl.program_id(0)

    @pl.when(step == 0)
    def _():
        own_ref[...] = jnp.zeros_like(own_ref)
        acc_ref[...] = jnp.zeros_like(acc_ref)
        for c in range(col_blocks):

            @pl.when(col_idx * col_blocks + c == 2 * z_idx + core_idx)
            def _():
                start = pl.multiple_of(z_idx * strip, strip)
                own_ref[pl.ds(start, strip), c * width : (c + 1) * width] = cam_ref[...]

    def build(part, row_ref, col_ref):
        for s in range(sources):
            aux = got_ref[s, base_aux : base_aux + AUX, :].astype(jnp.float32)
            vis = [aux[k : k + 1, :] for k in range(slots)]
            inv = [aux[slots + e : slots + e + 1, :] for e in range(6)]

            def picks_of(block, one):
                block = block.astype(jnp.float32)
                return [jnp.where(v == block, one, 0.0).astype(jnp.bfloat16) for v in vis]

            col_picks = [picks_of(col_idx * col_blocks + c, 1.0) for c in range(col_blocks)]
            for h in range(0, width // parts, fine):
                terms = []
                for at in range(3 * slots):
                    start = pl.multiple_of(at * width + part * (width // parts) + h, fine)
                    terms.append(got_ref[s, pl.ds(start, fine), :])
                for c in range(col_blocks):
                    rows = [chosen(col_picks[c], terms[a::3]).astype(jnp.float32) for a in range(3)]
                    start = pl.multiple_of(c * width + part * (width // parts) + h, fine)
                    for a, z in enumerate(apply_inverse(inv, rows)):
                        at = (a * sources + s) * points
                        col_ref[pl.ds(start, fine), at : at + points] = z.astype(jnp.bfloat16)
            deep = strip // parts
            terms = []
            for at in range(3 * slots):
                start = pl.multiple_of(at * width + row_idx * strip + part * deep, deep)
                terms.append(got_ref[s, pl.ds(start, deep), :])
            for b in range(blocks):
                other = b >= blocks // 2
                picks = picks_of(2 * (b % (blocks // 2)) + (1 - core_idx if other else core_idx), -1.0)
                start = pl.multiple_of(b * strip + part * deep, deep)
                for a in range(3):
                    at = (a * sources + s) * points
                    row_ref[pl.ds(start, deep), at : at + points] = chosen(picks, terms[a::3])

    def multiply(part, row_ref, col_ref):
        span = col_count // parts
        cols = pl.ds(pl.multiple_of(part * span, span), span)
        terms = lax.dot_general(row_ref[...], col_ref[cols, :], NT, preferred_element_type=jnp.float32)
        own_ref[:, cols] += terms[:half]
        acc_ref[:, cols] += terms[half:]

    even, odd = operands[:2], operands[2:]

    @pl.when(step == 0)
    def _():
        @pl.loop(0, parts)
        def _(part):
            build(part, *even)

    for parity, ready, coming in ((1, even, odd), (0, odd, even)):

        @pl.when((step > 0) & (step % 2 == parity))
        def _():
            @pl.loop(0, parts)
            def _(part):
                multiply(part, *ready)
                build(part, *coming)

    @pl.when(step == pl.num_programs(0) - 1)
    def _():
        peer_ref[...] = acc_ref[...].astype(jnp.bfloat16)


def tree(values):
    while len(values) > 1:
        values = [values[i] + values[i + 1] for i in range(0, len(values), 2)]
    return values[0]


def core_sum(value):
    return value + lax.ppermute(value, "core", [(0, 1), (1, 0)])


def all_sum(value, n_z, n_row, n_col):
    value = core_sum(value)
    far = n_z // 2
    pairs = [[(2 * z + c, 2 * (z ^ (j + c * far)) + c) for z in range(n_z) for c in range(2)] for j in range(far)]
    value = tree([lax.ppermute(value, ("z", "core"), p) for p in pairs])
    for axis, size in (("row", n_row), ("col", n_col)):
        swaps = [lax.ppermute(value, axis, [(i, i ^ b) for i in range(size)]) for b in range(1, size)]
        value = tree([value] + swaps)
    return core_sum(value)


def per_device(weights, visibility, inverses, grad_points, camera_blocks, grad_cams):
    n_row = lax.axis_size("row")
    n_col = lax.axis_size("col")
    n_z = lax.axis_size("z")
    blocks = 2 * n_z
    z_idx = lax.axis_index("z")
    core_idx = lax.axis_index("core")
    pts_idx = 2 * z_idx + core_idx
    row_idx = lax.axis_index("row")
    col_idx = lax.axis_index("col")
    slots, points = visibility.shape
    width = weights.shape[2]
    strip = width // n_row
    total_rows = blocks * width
    col_count = total_rows // n_col
    set_rows = blocks * strip
    shards = n_row * n_col
    send_rows = 3 * slots * width + AUX
    place = jnp.stack([z_idx, core_idx, row_idx, col_idx]).astype(jnp.int32)
    w_flat = weights.reshape(3 * slots * points, width)
    first_col = (col_idx == 0).astype(jnp.float32)
    lanes = jnp.arange(width, dtype=jnp.int32)[None, :]
    own_lanes = (lanes // strip == row_idx) & (jnp.arange(blocks, dtype=jnp.int32)[:, None] == pts_idx)
    cams_placed = jnp.where(own_lanes, jnp.tile(grad_cams, n_row)[None, :] * first_col, 0.0)
    cam_wide = lax.dynamic_update_slice(
        jnp.zeros((width, width), jnp.float32), camera_blocks * first_col, (row_idx * strip, 0)
    )
    vmem = pl.BlockSpec(memory_space=pltpu.VMEM)
    smem = pl.BlockSpec(memory_space=pltpu.SMEM)
    vec = jax.ShapeDtypeStruct((blocks, width), jnp.float32)
    small = pltpu.CompilerParams(vmem_limit_bytes=16 * 1024 * 1024)

    send = pl.pallas_call(
        functools.partial(send_kernel, slots),
        out_shape=jax.ShapeDtypeStruct((send_rows, points), jnp.bfloat16),
        in_specs=[pl.BlockSpec(memory_space=pl.ANY), vmem, vmem],
        out_specs=pl.BlockSpec(memory_space=pl.ANY),
        scratch_shapes=[
            pltpu.VMEM((3 * slots * points, width), jnp.bfloat16),
            pltpu.VMEM((send_rows, points), jnp.bfloat16),
            pltpu.SemaphoreType.DMA((slots,)),
            pltpu.SemaphoreType.DMA((slots + 1,)),
        ],
        name="send",
    )(w_flat, visibility, inverses)
    got = lax.all_gather(send, ("row", "col"), axis=0, tiled=False)
    zw, part = pl.pallas_call(
        functools.partial(prepare_kernel, slots, blocks),
        out_shape=(jax.ShapeDtypeStruct((width, 3 * slots * points), jnp.bfloat16), vec),
        in_specs=[vmem] * 5,
        out_specs=(vmem, vmem),
        compiler_params=small,
        name="prepare",
    )(w_flat, visibility, inverses, grad_points, cams_placed)

    def product(known):
        return pl.pallas_call(
            functools.partial(product_kernel, slots, blocks, len(known)),
            out_shape=vec,
            in_specs=[smem] + [vmem] * (4 + len(known)),
            out_specs=vmem,
            compiler_params=small,
            name="product",
        )(place, visibility, w_flat, zw, cam_wide, *known)

    pair = 2
    half = set_rows // 2
    steps = shards // pair
    make_halves = pl.pallas_call(
        functools.partial(tile_kernel, slots, blocks, width, strip, 2),
        out_shape=(
            jax.ShapeDtypeStruct((half, col_count), jnp.float32),
            jax.ShapeDtypeStruct((half, col_count), jnp.bfloat16),
        ),
        grid=(steps + 1,),
        in_specs=[
            smem,
            pl.BlockSpec((pair, send_rows, points), lambda i: (jnp.minimum(i, steps - 1), 0, 0)),
            pl.BlockSpec((strip, width), lambda i: (0, 0)),
        ],
        out_specs=(
            pl.BlockSpec((half, col_count), lambda i: (0, 0)),
            pl.BlockSpec((half, col_count), lambda i: (0, 0)),
        ),
        scratch_shapes=[
            pltpu.VMEM((half, col_count), jnp.float32),
            pltpu.VMEM((set_rows, 3 * pair * points), jnp.bfloat16),
            pltpu.VMEM((col_count, 3 * pair * points), jnp.bfloat16),
            pltpu.VMEM((set_rows, 3 * pair * points), jnp.bfloat16),
            pltpu.VMEM((col_count, 3 * pair * points), jnp.bfloat16),
        ],
        compiler_params=pltpu.CompilerParams(
            dimension_semantics=("arbitrary",), vmem_limit_bytes=50 * 1024 * 1024
        ),
        cost_estimate=pl.CostEstimate(
            flops=2 * set_rows * col_count * 3 * shards * points,
            bytes_accessed=2 * shards * send_rows * points + 4 * set_rows * col_count,
            transcendentals=0,
        ),
        name="tile",
    )

    known = [all_sum(part, n_z, n_row, n_col)]
    for _ in range(1, ITERS):
        known.append(all_sum(product(known), n_z, n_row, n_col))
    got, known = lax.optimization_barrier((got, known))
    own_half, peer_half = make_halves(place, got, camera_blocks)
    taken = lax.ppermute(peer_half, "core", [(0, 1), (1, 0)])
    tile, known = lax.optimization_barrier((own_half + taken.astype(jnp.float32), known))
    schur = lax.psum_scatter(tile, "z", scatter_dimension=0, tiled=True)
    known.append(all_sum(product(known), n_z, n_row, n_col))
    own = jax.ShapeDtypeStruct((1, strip), jnp.float32)
    own_rhs, answer = pl.pallas_call(
        functools.partial(answer_kernel, strip),
        out_shape=(own, own),
        in_specs=[smem] + [vmem] * 4,
        out_specs=(vmem, vmem),
        compiler_params=small,
        name="answer",
    )(place, *known)
    return (schur, own_rhs.reshape(strip), answer.reshape(strip))


def solution(mesh):
    n_pts, n_row, n_col = (mesh.shape[axis] for axis in ("pts", "row", "col"))
    cores = Mesh(mesh.devices.reshape(n_pts // 2, 2, n_row, n_col), ("z", "core", "row", "col"))
    pts = ("z", "core")
    return jax.shard_map(
        per_device,
        mesh=cores,
        in_specs=(
            P(None, (*pts, "row", "col"), None),
            P(None, (*pts, "row", "col")),
            P(None, (*pts, "row", "col")),
            P(None, (*pts, "row", "col")),
            P((*pts, "row"), None),
            P((*pts, "row")),
        ),
        out_specs=(P((*pts, "row"), "col"), P((*pts, "row")), P((*pts, "row"))),
        check_vma=False,
    )
```
